32 devices in a mesh: fsdp: 8 (over y, x, core), seq: 4 (over z).
Axes of the slice: x: 2, y: 2, z: 4, core: 2. Of those that a mesh axis runs over, the one named last changes fastest.
Arguments:
- inputs: float32 [4096, 768], P(('fsdp', 'seq')), may hold values from -6 to 6
- qkv_weight: bfloat16 [768, 2304], P(('fsdp', 'seq')), may hold values from -8 to 8
- proj_weight: bfloat16 [768, 768], P(('fsdp', 'seq')), may hold values from -2.5 to 2.5
- first_gain: bfloat16 [768], P(('fsdp', 'seq')), may hold values from 0.5 to 1.5
- first_shift: bfloat16 [768], P(('fsdp', 'seq')), may hold values from -3 to 3
- second_gain: bfloat16 [768], P(('fsdp', 'seq')), may hold values from 0.5 to 1.5
- second_shift: bfloat16 [768], P(('fsdp', 'seq')), may hold values from -3 to 3
- expert_up: bfloat16 [8, 768, 3072], P('fsdp', None, 'seq'), may hold values from -0.21875 to 0.21875
- expert_down: bfloat16 [8, 768, 3072], P('fsdp', None, 'seq'), may hold values from -0.109375 to 0.109375
- gate_logits: float32 [4096, 2], P(('fsdp', 'seq')), may hold values from -160 to 160
- routes: int32 [4096, 2], P(('fsdp', 'seq')), may hold values from 0 to 7, all different within a row; in each aligned block of 128 rows (0 to 127, 128 to 255, ...) at most 64 rows name the same one
- cotangent: float32 [4096, 768], P(('fsdp', 'seq')), may hold values from -6 to 6
Outputs:
- output: float32 [4096, 768], P(('fsdp', 'seq'))
- grad_inputs: float32 [4096, 768], P(('fsdp', 'seq'))
- grad_qkv_weight: float32 [768, 2304], P(('fsdp', 'seq'))
- grad_proj_weight: float32 [768, 768], P(('fsdp', 'seq'))
- grad_first_gain: float32 [768], P(('fsdp', 'seq'))
- grad_first_shift: float32 [768], P(('fsdp', 'seq'))
- grad_second_gain: float32 [768], P(('fsdp', 'seq'))
- grad_second_shift: float32 [768], P(('fsdp', 'seq'))
- grad_expert_up: float32 [8, 768, 3072], P('fsdp', None, 'seq')
- grad_expert_down: float32 [8, 768, 3072], P('fsdp', None, 'seq')
The draws below stay inside these ranges and needn't reach their ends.
Inputs may be any that keep to these rules, and one draw needn't show every extreme that they name: `routes`: each row names 2 different experts. In each aligned block of 128 rows (the rows of one device) no expert is named by more than 64 rows, a bound that some block reaches.
All inputs are finite; a program needn't handle non-finite values.
Results may differ from the reference program's by a relative error of at most 0.012.
Values may be sent and summed in bfloat16 or wider, within the bound.
No kernel may reach another device: no remote copies, remote signals or barrier semaphores. Data moves between devices by JAX's collectives and lax.ppermute only.
A program may use at most 128 MiB of HBM per device.

```python
import math
import jax
import jax.numpy as jnp
import numpy as np
from jax import lax

D = 768
HEADS = 12
HD = 64
FF = 3072
TOP = 2
TOK_DEV = 128
EXPERTS = 8
LEN = 512
TOKENS = 4096
CAP = 64
N_FSDP = 8
N_SEQ = 4


def draw_qkv_weight(key, part):
    base_key = jax.random.fold_in(key, 0)
    columns = jax.random.normal(base_key, (D, 3, HEADS, HD), jnp.float32) * D ** (-0.5)
    columns = jnp.clip(columns, -8.0, 8.0)
    return columns.reshape(D, 3 * D).astype(jnp.bfloat16)


def draw_gate_logits(key, part):
    pair_key = jax.random.fold_in(key, 0)
    logits = jax.random.normal(pair_key, (TOKENS, TOP), jnp.float32) * 1.5
    return jnp.clip(logits, -160.0, 160.0)


def shard_levels(stream_key, shape, cuts, low, high):
    factor_of = 1.0
    for axis_at, shards_of in cuts:
        draws = jax.random.uniform(jax.random.fold_in(jax.random.fold_in(stream_key, 6), axis_at), (shards_of,), jnp.float32, low / len(cuts), high / len(cuts))
        factor_of = factor_of * jnp.repeat(jnp.exp(draws), shape[axis_at] // shards_of).reshape((-1,) + (1,) * (len(shape) - 1 - axis_at))
    return factor_of


def assign_block(own_key, own, number, rows, amount, top, most, lean):
    ranking = jax.random.permutation(own_key, amount)
    packed, usual = load_shares(amount, rows * top, most, lean, True), load_shares(amount, rows * top, most, lean, False)
    places = jnp.arange(amount)

    def named(sizes, offset_by):
        used = int((sizes > 0).sum())
        fixed = max(1, used // 4)
        shifted = fixed + (places - fixed + offset_by * (used - fixed)) % max(1, amount - fixed)
        return jnp.zeros((amount,), jnp.int32).at[ranking[jnp.where(places < fixed, places, shifted)]].set(jnp.asarray(sizes, jnp.int32))

    sizes = jnp.where(number % 4 == 0, named(packed, number // 4), named(usual, number - number // 4 - 1))
    mixed = jax.random.permutation(jax.random.fold_in(own, 3), amount)
    giver, taker = mixed[0:amount // 2 * 2:2], mixed[1:amount // 2 * 2:2]
    room = jnp.minimum(sizes[giver] - 1, most - sizes[taker]) // 2
    room = jnp.where((giver == ranking[0]) | (taker == ranking[0]) | (sizes[taker] == 0), 0, jnp.maximum(room, 0))
    shifted = jax.random.randint(jax.random.fold_in(own, 4), (amount // 2,), 0, 1 << 20) % (room + 1)
    sizes = sizes.at[giver].add(-shifted).at[taker].add(shifted)
    items = jnp.searchsorted(jnp.cumsum(sizes), jnp.arange(rows * top), side="right").astype(jnp.int32)
    listing = items.reshape(top, rows).T
    listing = listing[jax.random.permutation(jax.random.fold_in(own, 1), rows)]
    offset_by = jax.random.randint(jax.random.fold_in(own, 2), (rows, 1), 0, top)
    return jnp.take_along_axis(listing, (jnp.arange(top)[None, :] + offset_by) % top, axis=1)


def load_shares(number_of, total, most, slope, full):
    weights = [(1 << 20) // math.isqrt(rank ** slope) + 1 for rank in range(1, number_of + 1)]
    largest = most if full else min(most, max(-(-total // number_of), total * weights[0] // sum(weights)))
    least = 1 if total - largest >= number_of - 1 else 0
    counts, surplus = [largest] + [least] * (number_of - 1), total - largest - least * (number_of - 1)
    while surplus > 0:
        free = [i for i in range(1, number_of) if counts[i] < largest] or [i for i in range(1, number_of) if counts[i] < most]
        pool, left = sum([weights[i] for i in free]), surplus
        for i in free:
            addition = min(most - counts[i], max(1, left * weights[i] // pool), surplus)
            counts[i] = counts[i] + addition
            surplus = surplus - addition
    return np.array(counts)


def gaussian(key, dims, deviation, limit, cuts=(), kind=jnp.bfloat16):
    array = jax.random.normal(key, dims, jnp.float32) * deviation
    if len(cuts) > 0:
        array = shard_levels(key, dims, cuts, -0.22, 0.18) * array
    return jnp.clip(array, min=-limit, max=limit).astype(kind)


def setup_inputs(seed: int = 0) -> dict:
    arg_keys = jax.random.split(jax.random.key(seed), 13)
    inputs = gaussian(arg_keys[0], (TOKENS, D), 1.0, 6.0, ((0, 32),), jnp.float32)
    qkv_weight = draw_qkv_weight(jax.random.fold_in(arg_keys[12], 71), 0)
    proj_weight = gaussian(arg_keys[2], (D, D), (max(4, 4 * D // LEN)) ** -0.5, 2.5, ((0, 32),))
    first_gain = jnp.clip(1.0 + 0.1 * jax.random.normal(arg_keys[3], (D,), jnp.float32), 0.5, 1.5).astype(jnp.bfloat16)
    first_shift = gaussian(arg_keys[4], (D,), 0.5, 3.0, ((0, 32),))
    second_gain = jnp.clip(1.0 + 0.1 * jax.random.normal(arg_keys[5], (D,), jnp.float32), 0.5, 1.5).astype(jnp.bfloat16)
    second_shift = gaussian(arg_keys[6], (D,), 0.5, 3.0, ((0, 32),))
    expert_up = gaussian(arg_keys[7], (EXPERTS, D, FF), D ** -0.5, 0.21875, ((0, 8), (2, 4)))
    expert_down = gaussian(arg_keys[8], (EXPERTS, D, FF), FF ** -0.5, 0.109375, ((0, 8), (2, 4)))
    gate_logits = draw_gate_logits(jax.random.fold_in(arg_keys[12], 71), 0)
    routes_keys = jax.random.split(jax.random.fold_in(arg_keys[10], 1), TOKENS // TOK_DEV)
    routes_turns = jax.random.permutation(jax.random.fold_in(arg_keys[10], 3), TOKENS // TOK_DEV)
    routes = jax.vmap(lambda own, number: assign_block(jax.random.fold_in(arg_keys[10], 2), own, number, TOK_DEV, EXPERTS, TOP, CAP, 2))(routes_keys, routes_turns).reshape((TOKENS, TOP))
    cotangent = gaussian(arg_keys[11], (TOKENS, D), 1.0, 6.0, ((0, 32),), jnp.float32)
    return {"inputs": inputs, "qkv_weight": qkv_weight, "proj_weight": proj_weight, "first_gain": first_gain, "first_shift": first_shift, "second_gain": second_gain, "second_shift": second_shift, "expert_up": expert_up, "expert_down": expert_down, "gate_logits": gate_logits, "routes": routes, "cotangent": cotangent}


epsilon = 1e-06

def layer_norm(rows_in, gain_row, shift_row):
    average = lax.optimization_barrier(jnp.mean(rows_in, axis=-1, keepdims=True))
    centred = rows_in - average
    spread = lax.optimization_barrier(jnp.mean(centred * centred, axis=-1, keepdims=True))
    return centred * lax.rsqrt(spread + epsilon) * gain_row + shift_row

def mix_float(form, left, right):
    return jnp.einsum(form, left.astype(jnp.float32), right.astype(jnp.float32), precision=lax.Precision.HIGHEST)

def attention_forward(q_rows, k_rows, v_rows):
    length = q_rows.shape[0]
    block_rows = min(512, length)
    score_scale = q_rows.shape[2] ** (-0.5)
    grouped = q_rows.reshape(length // block_rows, block_rows, q_rows.shape[1], q_rows.shape[2])

    def one_block(q_block):
        scores = mix_float('qhd,khd->hqk', q_block, k_rows) * score_scale
        top_score = lax.optimization_barrier(jnp.max(scores, axis=-1, keepdims=True))
        weights = jnp.exp(scores - top_score)
        totals = lax.optimization_barrier(jnp.sum(weights, axis=-1, keepdims=True))
        probs_low = (weights / totals).astype(jnp.bfloat16)
        result = mix_float('hqk,khd->qhd', probs_low, v_rows).astype(jnp.bfloat16)
        return (result, (top_score + jnp.log(totals))[..., 0])
    results, log_totals = lax.map(one_block, grouped)
    return (results.reshape(q_rows.shape), log_totals)

def attention_backward(q_rows, k_rows, v_rows, log_totals, grad_out):
    length = q_rows.shape[0]
    block_rows = min(512, length)
    score_scale = q_rows.shape[2] ** (-0.5)
    grouped_q = q_rows.reshape(length // block_rows, block_rows, q_rows.shape[1], q_rows.shape[2])
    grouped_g = grad_out.reshape(grouped_q.shape)

    def one_block(running, pieces):
        grad_k, grad_v = running
        q_block, g_block, lse_block = pieces
        scores = mix_float('qhd,khd->hqk', q_block, k_rows) * score_scale
        probs_full = jnp.exp(scores - lse_block[..., None])
        probs_low = probs_full.astype(jnp.bfloat16)
        grad_v = grad_v + mix_float('hqk,qhd->khd', probs_low, g_block)
        grad_p = mix_float('qhd,khd->hqk', g_block, v_rows)
        row_dot = lax.optimization_barrier(jnp.sum(probs_full * grad_p, axis=-1, keepdims=True))
        grad_s = (probs_full * (grad_p - row_dot) * score_scale).astype(jnp.bfloat16)
        grad_q = mix_float('hqk,khd->qhd', grad_s, k_rows).astype(jnp.bfloat16)
        grad_k = grad_k + mix_float('hqk,qhd->khd', grad_s, q_block)
        return ((grad_k, grad_v), grad_q)
    empty_grad = jnp.zeros(k_rows.shape, jnp.float32)
    (grad_k, grad_v), grad_q = lax.scan(one_block, (empty_grad, empty_grad), (grouped_q, grouped_g, log_totals))
    return (grad_q.reshape(q_rows.shape), grad_k.astype(jnp.bfloat16), grad_v.astype(jnp.bfloat16))

def slot_table(routes, experts, capacity):
    flat_ids = routes.reshape(-1)
    labels = jnp.arange(experts, dtype=jnp.int32)
    onehot = (flat_ids[:, None] == labels[None, :]).astype(jnp.int32)
    before = jnp.cumsum(onehot, axis=0) - onehot
    return (flat_ids * capacity + lax.optimization_barrier(jnp.sum(before * onehot, axis=1))).astype(jnp.int32)

def place_rows(entries, slot_ids, slot_count):
    return jnp.zeros((slot_count, entries.shape[1]), entries.dtype).at[slot_ids].set(entries)

def expert_forward(rows_in, up_mat, down_mat):
    pre_act = jnp.dot(rows_in, up_mat, preferred_element_type=jnp.float32)
    hidden = jax.nn.gelu(pre_act).astype(jnp.bfloat16)
    result = lax.dot_general(hidden, down_mat, (((1,), (1,)), ((), ())), preferred_element_type=jnp.float32)
    return (pre_act, hidden, result)

def expert_backward(rows_in, pre_act, hidden, grad_out, up_mat, down_mat):
    grad_hidden = jnp.dot(grad_out, down_mat, preferred_element_type=jnp.float32)
    _, gelu_back = jax.vjp(jax.nn.gelu, pre_act)
    grad_pre = gelu_back(grad_hidden)[0].astype(jnp.bfloat16)
    grad_down = lax.dot_general(grad_out, hidden, (((0,), (0,)), ((), ())), preferred_element_type=jnp.float32)
    grad_up = lax.dot_general(rows_in, grad_pre, (((0,), (0,)), ((), ())), preferred_element_type=jnp.float32)
    grad_rows = lax.dot_general(grad_pre, up_mat, (((1,), (1,)), ((), ())), preferred_element_type=jnp.float32)
    return (grad_rows, grad_up, grad_down)

def reference(inputs, qkv_weight, proj_weight, first_gain, first_shift, second_gain, second_shift, expert_up, expert_down, gate_logits, routes, cotangent):
    gain_one = first_gain.astype(jnp.float32)
    shift_one = first_shift.astype(jnp.float32)
    gain_two = second_gain.astype(jnp.float32)
    shift_two = second_shift.astype(jnp.float32)
    attn_in = layer_norm(inputs, gain_one, shift_one).astype(jnp.bfloat16)
    qkv = jnp.dot(attn_in, qkv_weight, preferred_element_type=jnp.float32).astype(jnp.bfloat16)
    qkv_images = qkv.reshape(N_FSDP, LEN, 3, HEADS, HD)

    def image_forward(pieces):
        return attention_forward(pieces[:, 0], pieces[:, 1], pieces[:, 2])
    heads_images, log_totals = lax.map(image_forward, qkv_images)
    heads_out = heads_images.reshape(TOKENS, D)
    residual = inputs + jnp.dot(heads_out, proj_weight, preferred_element_type=jnp.float32)
    ffn_in = layer_norm(residual, gain_two, shift_two).astype(jnp.bfloat16)
    top_logit = lax.optimization_barrier(jnp.max(gate_logits, axis=1, keepdims=True))
    raised = jnp.exp(gate_logits - top_logit)
    gate_probs = raised / lax.optimization_barrier(jnp.sum(raised, axis=1, keepdims=True))
    block_count = N_FSDP * N_SEQ
    slot_count = EXPERTS * CAP
    slot_ids = jax.vmap(lambda part_routes: slot_table(part_routes, EXPERTS, CAP))(routes.reshape(block_count, TOK_DEV, TOP))
    repeated = jnp.repeat(ffn_in, TOP, axis=0).reshape(block_count, TOK_DEV * TOP, D)
    sent = jax.vmap(lambda entries, ids: place_rows(entries, ids, slot_count))(repeated, slot_ids)
    grad_entry = (gate_probs[:, :, None] * cotangent[:, None, :]).astype(jnp.bfloat16)
    grad_sent = jax.vmap(lambda entries, ids: place_rows(entries, ids, slot_count))(grad_entry.reshape(block_count, TOK_DEV * TOP, D), slot_ids)

    def to_expert_major(buffer):
        return buffer.reshape(block_count, EXPERTS, CAP, D).transpose(1, 0, 2, 3).reshape(EXPERTS, block_count * CAP, D)

    def to_block_major(buffer):
        return buffer.reshape(EXPERTS, block_count, CAP, D).transpose(1, 0, 2, 3).reshape(block_count, slot_count, D)

    def expert_pass(pieces):
        rows_in, grad_out, up_mat, down_mat = pieces
        pre_act, hidden, produced = expert_forward(rows_in, up_mat, down_mat)
        grad_rows, grad_up, grad_down = expert_backward(rows_in, pre_act, hidden, grad_out, up_mat, down_mat)
        return (produced.astype(jnp.bfloat16), grad_rows.astype(jnp.bfloat16), grad_up, grad_down)
    expert_out, grad_rows, grad_expert_up, grad_expert_down = lax.map(expert_pass, (to_expert_major(sent), to_expert_major(grad_sent), expert_up, expert_down))
    picked = jax.vmap(lambda buffer, ids: buffer[ids])(to_block_major(expert_out), slot_ids).reshape(TOKENS, TOP, D)
    output = residual + lax.optimization_barrier(jnp.sum(gate_probs[:, :, None] * picked.astype(jnp.float32), axis=1))
    grad_picked = jax.vmap(lambda buffer, ids: buffer[ids])(to_block_major(grad_rows), slot_ids).reshape(TOKENS, TOP, D)
    grad_ffn_in = lax.optimization_barrier(jnp.sum(grad_picked.astype(jnp.float32), axis=1))
    _, second_back = jax.vjp(layer_norm, residual, gain_two, shift_two)
    grad_from_ffn, grad_second_gain, grad_second_shift = second_back(grad_ffn_in)
    grad_residual = cotangent + grad_from_ffn
    grad_mix = grad_residual.astype(jnp.bfloat16)
    grad_proj_weight = lax.dot_general(heads_out, grad_mix, (((0,), (0,)), ((), ())), preferred_element_type=jnp.float32)
    grad_heads = lax.dot_general(grad_mix, proj_weight, (((1,), (1,)), ((), ())), preferred_element_type=jnp.float32).astype(jnp.bfloat16)

    def image_backward(pieces):
        image_qkv, image_lse, image_grad = pieces
        return attention_backward(image_qkv[:, 0], image_qkv[:, 1], image_qkv[:, 2], image_lse, image_grad)
    grad_q, grad_k, grad_v = lax.map(image_backward, (qkv_images, log_totals, grad_heads.reshape(N_FSDP, LEN, HEADS, HD)))
    grad_qkv = jnp.stack([grad_q, grad_k, grad_v], axis=2).reshape(TOKENS, 3 * D)
    grad_qkv_weight = lax.dot_general(attn_in, grad_qkv, (((0,), (0,)), ((), ())), preferred_element_type=jnp.float32)
    grad_attn_in = lax.dot_general(grad_qkv, qkv_weight, (((1,), (1,)), ((), ())), preferred_element_type=jnp.float32)
    _, first_back = jax.vjp(layer_norm, inputs, gain_one, shift_one)
    grad_from_attn, grad_first_gain, grad_first_shift = first_back(grad_attn_in)
    grad_inputs = grad_residual + grad_from_attn
    return (output, grad_inputs, grad_qkv_weight, grad_proj_weight, grad_first_gain, grad_first_shift, grad_second_gain, grad_second_shift, grad_expert_up, grad_expert_down)
```

```python
import functools

import jax
import jax.numpy as jnp
from jax import lax
from jax.experimental import pallas as pl
from jax.experimental.pallas import tpu as pltpu
from jax.sharding import PartitionSpec as P

HD = 64
EPS = 1e-06
BF = jnp.bfloat16
F32 = jnp.float32
C0 = 0.7978845608028654
C1 = 0.044715


def mm(a, b):
    return jnp.dot(a, b, preferred_element_type=F32)


def mm_nt(a, b):
    return lax.dot_general(a, b, (((1,), (1,)), ((), ())), preferred_element_type=F32)


def mm_tn(a, b):
    return lax.dot_general(a, b, (((0,), (0,)), ((), ())), preferred_element_type=F32)


def kernel_call(body, outs, args, name, smem=0, scratch=()):
    vm = pl.BlockSpec(memory_space=pltpu.VMEM)
    sm = pl.BlockSpec(memory_space=pltpu.SMEM)
    return pl.pallas_call(
        body,
        out_shape=[jax.ShapeDtypeStruct(s, d) for s, d in outs],
        in_specs=[sm] * smem + [vm] * (len(args) - smem),
        out_specs=[vm] * len(outs),
        scratch_shapes=list(scratch),
        name=name,
    )(*args)


def exchange(chunks, axis, count):
    got = [chunks[0]]
    for d in range(1, count):
        got.append(lax.ppermute(chunks[d], axis, [(i, i ^ d) for i in range(count)]))
    return got


def norm_parts(x):
    mean = jnp.mean(x, axis=-1, keepdims=True)
    centred = x - mean
    spread = jnp.mean(centred * centred, axis=-1, keepdims=True)
    scale = lax.rsqrt(spread + EPS)
    return centred * scale, scale


def norm_back(x, gain, dy):
    hat, scale = norm_parts(x)
    dhat = dy * gain
    a = jnp.mean(dhat, axis=-1, keepdims=True)
    b = jnp.mean(dhat * hat, axis=-1, keepdims=True)
    dx = scale * (dhat - a - hat * b)
    return dx, jnp.sum(dy * hat, axis=0, keepdims=True), jnp.sum(dy, axis=0, keepdims=True)


def first_norm_body(x_ref, gains_ref, out_ref):
    hat, _ = norm_parts(x_ref[...])
    out_ref[...] = (hat * gains_ref[0:1, :] + gains_ref[1:2, :]).astype(BF)


def attention_forward_body(heads, a_ref, w_ref, qkv_ref, out_ref, lse_ref):
    group = heads * HD
    qkv_ref[...] = mm(a_ref[...], w_ref[...]).astype(BF)
    for h in range(heads):
        q = qkv_ref[:, h * HD : (h + 1) * HD]
        k = qkv_ref[:, group + h * HD : group + (h + 1) * HD]
        v = qkv_ref[:, 2 * group + h * HD : 2 * group + (h + 1) * HD]
        scores = mm_nt(q, k) * HD ** (-0.5)
        top = jnp.max(scores, axis=-1, keepdims=True)
        weights = jnp.exp(scores - top)
        total = jnp.sum(weights, axis=-1, keepdims=True)
        probs = (weights / total).astype(BF)
        out_ref[:, h * HD : (h + 1) * HD] = mm(probs, v).astype(BF)
        lse_ref[:, h : h + 1] = top + jnp.log(total)


def attention_backward_body(
    heads, me_ref, mix_ref, proj_ref, qkv_ref, lse_ref, w_ref, gqkv_ref, own_ref, send_ref, part_ref
):
    group = heads * HD
    scale = HD ** (-0.5)
    grad_heads = mm_nt(mix_ref[...], proj_ref[...]).astype(BF)
    for h in range(heads):
        q = qkv_ref[:, h * HD : (h + 1) * HD]
        k = qkv_ref[:, group + h * HD : group + (h + 1) * HD]
        v = qkv_ref[:, 2 * group + h * HD : 2 * group + (h + 1) * HD]
        g = grad_heads[:, h * HD : (h + 1) * HD]
        probs = jnp.exp(mm_nt(q, k) * scale - lse_ref[:, h : h + 1])
        grad_p = mm_nt(g, v)
        dots = jnp.sum(probs * grad_p, axis=-1, keepdims=True)
        grad_s = (probs * (grad_p - dots) * scale).astype(BF)
        gqkv_ref[:, h * HD : (h + 1) * HD] = mm(grad_s, k).astype(BF)
        gqkv_ref[:, group + h * HD : group + (h + 1) * HD] = mm_tn(grad_s, q).astype(BF)
        gqkv_ref[:, 2 * group + h * HD : 2 * group + (h + 1) * HD] = mm_tn(
            probs.astype(BF), g
        ).astype(BF)
    parts, rows, width = part_ref.shape
    part_ref[...] = mm_nt(gqkv_ref[...], w_ref[...]).reshape(parts, rows, width)
    spread_parts(me_ref[1], part_ref, own_ref, send_ref)


def spread_parts(me, part_ref, own_ref, send_ref):
    own_ref[...] = part_ref[me]
    for d in range(1, part_ref.shape[0]):
        send_ref[d - 1] = part_ref[me ^ d].astype(BF)


def weight_grad_body(a_ref, gqkv_ref, heads_ref, mix_ref, wq_ref, wp_ref):
    wq_ref[...] = mm_tn(a_ref[...], gqkv_ref[...]).astype(BF)
    wp_ref[...] = mm_tn(heads_ref[...], mix_ref[...]).astype(BF)


def project_body(count, me_ref, heads_ref, x_ref, gains_ref, *rest):
    chunk_refs = rest[:count]
    res_ref, ffn_ref, proj_s_ref, proj_ref = rest[count:]
    rows = chunk_refs[0].shape[0]
    for d in range(count):
        start = pl.multiple_of((me_ref[0] ^ d) * rows, rows)
        proj_ref[pl.ds(start, rows), :] = chunk_refs[d][...]
    groups, _, width = heads_ref.shape
    acc = x_ref[...]
    for s in range(groups):
        acc = acc + mm(heads_ref[s], proj_ref[s * width : (s + 1) * width, :])
    res_ref[...] = acc
    hat, _ = norm_parts(acc)
    ffn_ref[...] = (hat * gains_ref[2:3, :] + gains_ref[3:4, :]).astype(BF)
    proj_s_ref[...] = proj_ref[pl.ds(pl.multiple_of(me_ref[1] * width, width), width), :]


def table_body(experts, me_ref, *refs):
    blocks = refs[:-3]
    pos_ref, gate_ref, all_ref = refs[-3:]
    count = len(blocks)
    for d in range(count):
        all_ref[me_ref[1] ^ d] = blocks[d][...]
    flat = jnp.concatenate([all_ref[j] for j in range(count)], axis=1)
    tokens = flat.shape[1]
    first, second = flat[0:1, :], flat[1:2, :]
    left, right = flat[2:3, :], flat[3:4, :]
    top = jnp.maximum(left, right)
    left, right = jnp.exp(left - top), jnp.exp(right - top)
    total = left + right
    left, right = left / total, right / total
    label = lax.broadcasted_iota(jnp.int32, (experts, tokens), 0).astype(F32)
    is_first, is_second = label == first, label == second
    hit = is_first | is_second
    earlier = lax.broadcasted_iota(jnp.int32, (tokens, tokens), 0) < lax.broadcasted_iota(
        jnp.int32, (tokens, tokens), 1
    )
    rank = mm(jnp.where(hit, 1.0, 0.0).astype(BF), jnp.where(earlier, 1.0, 0.0).astype(BF))
    pos_ref[...] = jnp.where(hit, rank, -1.0)
    gate_ref[...] = jnp.where(is_first, left, 0.0) + jnp.where(is_second, right, 0.0)


def selection(pos_row, slots):
    tokens = pos_row.shape[1]
    slot = lax.broadcasted_iota(jnp.int32, (slots, tokens), 0).astype(F32)
    return slot == pos_row


def dispatch_body(experts, me_ref, pos_ref, tok_ref, *out_refs):
    slots = out_refs[0].shape[0]
    for d in range(experts):
        chosen = selection(pos_ref[pl.ds(me_ref[0] ^ d, 1), :], slots)
        pick = jnp.where(chosen, 1.0, 0.0).astype(BF)
        out_refs[d][...] = mm(pick, tok_ref[...]).astype(BF)


def dispatch_grad_body(experts, count, me_ref, pos_ref, gate_ref, *refs):
    blocks = refs[:count]
    out_refs = refs[count:-1]
    tok_ref = refs[-1]
    rows = blocks[0].shape[0]
    slots = out_refs[0].shape[0]
    for d in range(count):
        tok_ref[pl.ds(pl.multiple_of((me_ref[1] ^ d) * rows, rows), rows), :] = blocks[d][...]
    for d in range(experts):
        chosen = selection(pos_ref[pl.ds(me_ref[0] ^ d, 1), :], slots)
        pick = jnp.where(chosen, 1.0, 0.0).astype(BF)
        gate = jnp.sum(
            jnp.where(chosen, gate_ref[pl.ds(me_ref[0] ^ d, 1), :], 0.0), axis=1, keepdims=True
        )
        out_refs[d][...] = (mm(pick, tok_ref[...]) * gate).astype(BF)


def combine_body(experts, gated, me_ref, pos_ref, gate_ref, *refs):
    back = refs[:experts]
    own_ref, send_ref, part_ref = refs[experts:]
    slots = back[0].shape[0]
    parts, rows, width = part_ref.shape
    for d in range(experts):
        chosen = selection(pos_ref[pl.ds(me_ref[0] ^ d, 1), :], slots)
        if gated:
            gate = jnp.where(chosen, gate_ref[pl.ds(me_ref[0] ^ d, 1), :], 0.0)
            high = gate.astype(BF)
            low = (gate - high.astype(F32)).astype(BF)
            piece = mm_tn(high, back[d][...]) + mm_tn(low, back[d][...])
        else:
            piece = mm_tn(jnp.where(chosen, 1.0, 0.0).astype(BF), back[d][...])
        piece = piece.reshape(parts, rows, width)
        part_ref[...] = piece if d == 0 else part_ref[...] + piece
    spread_parts(me_ref[1], part_ref, own_ref, send_ref)


def hidden_grad_body(count, *refs):
    down_ref, out_ref = refs[count:]
    rows = refs[0].shape[0]
    for i in range(count):
        out_ref[i * rows : (i + 1) * rows, :] = mm(refs[i][...], down_ref[...])


def expert_body(count, *refs):
    rows_refs = refs[:count]
    gh_ref, up_ref = refs[count : count + 2]
    gr_refs = refs[count + 2 : 2 * count + 2]
    hid_ref, gp_ref = refs[2 * count + 2 :]
    rows = rows_refs[0].shape[0]
    for i in range(count):
        u = mm(rows_refs[i][...], up_ref[...])
        sq = u * u
        t = jnp.tanh(C0 * (u + C1 * (sq * u)))
        half = 0.5 * (1.0 + t)
        hid_ref[i * rows : (i + 1) * rows, :] = (u * half).astype(BF)
        slope = half + 0.5 * u * (1.0 - t * t) * (C0 * (1.0 + 3.0 * C1 * sq))
        gp_ref[i * rows : (i + 1) * rows, :] = (
            gh_ref[i * rows : (i + 1) * rows, :] * slope
        ).astype(BF)
        gr_refs[i][...] = mm_nt(gp_ref[i * rows : (i + 1) * rows, :], up_ref[...]).astype(BF)


def expert_out_body(count, hid_ref, down_ref, *out_refs):
    rows = out_refs[0].shape[0]
    for i in range(count):
        out_refs[i][...] = mm_nt(hid_ref[i * rows : (i + 1) * rows, :], down_ref[...]).astype(BF)


def expert_weight_body(count, groups, *refs):
    lefts, rights, out_ref = refs[: count * groups], refs[count * groups : -1], refs[-1]
    rows = lefts[0].shape[0]
    for g in range(groups):
        for i in range(count):
            piece = mm_tn(lefts[g * count + i][...], rights[g][i * rows : (i + 1) * rows, :])
            if g == 0 and i == 0:
                out_ref[0] = piece
            else:
                out_ref[0] += piece


def second_back_body(got_ref, own_ref, res_ref, cot_ref, gains_ref, grad_ref, mix_ref, sums_ref):
    dy = own_ref[...]
    for j in range(got_ref.shape[0]):
        dy = dy + got_ref[j].astype(F32)
    dx, dg, db = norm_back(res_ref[...], gains_ref[2:3, :], dy)
    grad = cot_ref[...] + dx
    grad_ref[...] = grad
    mix_ref[...] = grad.astype(BF)
    sums_ref[0:1, :] = dg
    sums_ref[1:2, :] = db


def first_back_body(count, *refs):
    got = refs[:count]
    own_ref, x_ref, gains_ref, res_ref, second_ref, out_ref, sums_ref = refs[count:]
    dy = own_ref[...]
    for j in range(count):
        dy = dy + got[j][...].astype(F32)
    dx, dg, db = norm_back(x_ref[...], gains_ref[0:1, :], dy)
    out_ref[...] = res_ref[...] + dx
    sums_ref[0:1, :] = dg
    sums_ref[1:2, :] = db
    sums_ref[2:4, :] = second_ref[...]


def local(
    inputs,
    qkv_weight,
    proj_weight,
    first_gain,
    first_shift,
    second_gain,
    second_shift,
    expert_up,
    expert_down,
    gate_logits,
    routes,
    cotangent,
):
    tok, width = inputs.shape
    ns = lax.axis_size("seq")
    nf = lax.axis_size("fsdp")
    group = width // ns
    heads = group // HD
    length = tok * ns
    slots = ns * (4 * tok // nf)
    wrows = qkv_weight.shape[0]
    cols = 3 * group
    hidden = expert_up.shape[2]
    me = jnp.stack([lax.axis_index("fsdp"), lax.axis_index("seq")]).astype(jnp.int32)
    groups = 4
    per = nf // groups

    info = jnp.concatenate([routes.astype(F32).T, gate_logits.T], axis=0)
    info = jnp.pad(info, ((0, 8 - info.shape[0]), (0, 0)))
    info_blocks = exchange([info] * ns, "seq", ns)

    by_group = qkv_weight.reshape(wrows, 3, ns, group).transpose(2, 0, 1, 3).reshape(ns, wrows, cols)
    gain_row = jnp.concatenate([first_gain, first_shift, second_gain, second_shift])
    gain_row = jnp.pad(gain_row, (0, cols - gain_row.shape[0]))
    packed = jnp.concatenate(
        [by_group, jnp.broadcast_to(gain_row[None, None, :], (ns, 1, cols))], axis=1
    )
    packed = lax.all_to_all(packed, "seq", split_axis=0, concat_axis=0, tiled=True)
    packed = lax.all_gather(packed, "fsdp", axis=0, tiled=True)
    qkv_w = packed[:, :wrows].reshape(width, cols)
    gains = (
        packed[:, wrows, : 4 * wrows]
        .reshape(nf * ns, 4, wrows)
        .transpose(1, 0, 2)
        .reshape(4, width)
        .astype(F32)
    )

    cot_blocks = exchange([cotangent.astype(BF)] * ns, "seq", ns)
    proj_rows = lax.all_gather(proj_weight, "seq", axis=0, tiled=True)
    proj_chunks = exchange([proj_rows] * nf, "fsdp", nf)

    (attn_own,) = kernel_call(
        first_norm_body, [((tok, width), BF)], (inputs, gains), "first_norm"
    )
    attn_in = lax.all_gather(attn_own, "seq", axis=0, tiled=True)
    qkv, heads_s, lse = kernel_call(
        functools.partial(attention_forward_body, heads),
        [((length, cols), BF), ((length, group), BF), ((length, 128), F32)],
        (attn_in, qkv_w),
        "attention_forward",
    )
    pos, gate = kernel_call(
        functools.partial(table_body, nf),
        [((nf, length), F32), ((nf, length), F32)],
        (me, *info_blocks),
        "tables",
        smem=1,
        scratch=[pltpu.VMEM((ns, 8, tok), F32)],
    )
    grad_sent = kernel_call(
        functools.partial(dispatch_grad_body, nf, ns),
        [((slots, width), BF)] * nf,
        (me, pos, gate, *cot_blocks),
        "dispatch_grad",
        smem=1,
        scratch=[pltpu.VMEM((length, width), BF)],
    )
    grad_in = exchange(grad_sent, "fsdp", nf)
    up, down = expert_up[0], expert_down[0]
    grad_hidden = [
        kernel_call(
            functools.partial(hidden_grad_body, per),
            [((per * slots, hidden), F32)],
            (*grad_in[g * per : (g + 1) * per], down),
            "hidden_grad",
        )[0]
        for g in range(groups)
    ]

    heads_own = lax.all_to_all(
        heads_s.reshape(ns, tok, group), "seq", split_axis=0, concat_axis=0, tiled=True
    )
    residual, ffn_own, proj_s = kernel_call(
        functools.partial(project_body, nf),
        [((tok, width), F32), ((tok, width), BF), ((group, width), BF)],
        (me, heads_own, inputs, gains, *proj_chunks),
        "project",
        smem=1,
        scratch=[pltpu.VMEM((width, width), BF)],
    )
    ffn_in = lax.all_gather(ffn_own, "seq", axis=0, tiled=True)
    sent = kernel_call(
        functools.partial(dispatch_body, nf),
        [((slots, width), BF)] * nf,
        (me, pos, ffn_in),
        "dispatch",
        smem=1,
    )
    rows_in = exchange(sent, "fsdp", nf)
    grad_rows, hid, grad_pre = [], [], []
    for g in range(groups):
        res = kernel_call(
            functools.partial(expert_body, per),
            [((slots, width), BF)] * per + [((per * slots, hidden), BF)] * 2,
            (*rows_in[g * per : (g + 1) * per], grad_hidden[g], up),
            "expert",
        )
        grad_rows += res[:per]
        hid.append(res[per])
        grad_pre.append(res[per + 1])
    grad_back = exchange(grad_rows, "fsdp", nf)
    expert_out = []
    for g in range(groups):
        expert_out += kernel_call(
            functools.partial(expert_out_body, per),
            [((slots, width), BF)] * per,
            (hid[g], down),
            "expert_out",
        )
    out_back = exchange(expert_out, "fsdp", nf)
    (grad_up,) = kernel_call(
        functools.partial(expert_weight_body, per, groups),
        [((1, width, hidden), F32)],
        (*rows_in, *grad_pre),
        "grad_up",
    )
    (grad_down,) = kernel_call(
        functools.partial(expert_weight_body, per, groups),
        [((1, width, hidden), F32)],
        (*grad_in, *hid),
        "grad_down",
    )

    combine_outs = [((tok, width), F32), ((ns - 1, tok, width), BF)]
    combine_scratch = [pltpu.VMEM((ns, tok, width), F32)]
    ffn_grad_own, ffn_grad_sent = kernel_call(
        functools.partial(combine_body, nf, False),
        combine_outs,
        (me, pos, gate, *grad_back),
        "combine_grad",
        smem=1,
        scratch=combine_scratch,
    )
    got = exchange([None] + [ffn_grad_sent[d] for d in range(ns - 1)], "seq", ns)[1:]
    grad_res, mix_own, sums_two = kernel_call(
        second_back_body,
        [((tok, width), F32), ((tok, width), BF), ((2, width), F32)],
        (jnp.stack(got), ffn_grad_own, residual, cotangent, gains),
        "second_back",
    )
    mix = lax.all_gather(mix_own, "seq", axis=0, tiled=True)
    grad_qkv, attn_grad_own, attn_grad_sent = kernel_call(
        functools.partial(attention_backward_body, heads),
        [((length, cols), BF)] + combine_outs,
        (me, mix, proj_s, qkv, lse, qkv_w),
        "attention_backward",
        smem=1,
        scratch=combine_scratch,
    )
    attn_got = exchange([None] + [attn_grad_sent[d] for d in range(ns - 1)], "seq", ns)[1:]
    part_q, part_p = kernel_call(
        weight_grad_body,
        [((width, cols), BF), ((group, width), BF)],
        (attn_in, grad_qkv, heads_s, mix),
        "weight_grad",
    )
    out_own, out_sent = kernel_call(
        functools.partial(combine_body, nf, True),
        combine_outs,
        (me, pos, gate, *out_back),
        "combine_out",
        smem=1,
        scratch=combine_scratch,
    )
    out_got = exchange([None] + [out_sent[d] for d in range(ns - 1)], "seq", ns)[1:]
    output = residual + out_own
    for piece in out_got:
        output = output + piece.astype(F32)
    grad_inputs, sums = kernel_call(
        functools.partial(first_back_body, ns - 1),
        [((tok, width), F32), ((4, width), F32)],
        (*attn_got, attn_grad_own, inputs, gains, grad_res, sums_two),
        "first_back",
    )

    def reduce_f(parts):
        parts = lax.all_to_all(parts, "fsdp", split_axis=0, concat_axis=0, tiled=True)
        return jnp.sum(parts.astype(F32), axis=0)

    sum_q = reduce_f(part_q.reshape(nf, ns * wrows, cols)).reshape(ns, wrows, cols)
    sum_q = lax.all_to_all(sum_q, "seq", split_axis=0, concat_axis=0, tiled=True)
    grad_qkv_weight = (
        sum_q.reshape(ns, wrows, 3, group).transpose(1, 2, 0, 3).reshape(wrows, 3 * width)
    )
    sum_p = reduce_f(part_p.reshape(nf, group // nf, width))
    grad_proj = lax.ppermute(
        sum_p,
        ("fsdp", "seq"),
        [(f * ns + s, s * nf + f) for f in range(nf) for s in range(ns)],
    )
    tiny = sums.reshape(4, nf, ns * wrows).transpose(1, 0, 2)
    tiny = jnp.sum(lax.all_to_all(tiny, "fsdp", split_axis=0, concat_axis=0, tiled=True), axis=0)
    tiny = tiny.reshape(4, ns, wrows).transpose(1, 0, 2)
    tiny = jnp.sum(lax.all_to_all(tiny, "seq", split_axis=0, concat_axis=0, tiled=True), axis=0)
    return (
        output,
        grad_inputs,
        grad_qkv_weight,
        grad_proj,
        tiny[0],
        tiny[1],
        tiny[2],
        tiny[3],
        grad_up,
        grad_down,
    )


def solution(mesh):
    both = ("fsdp", "seq")
    rows, line, expert = P(both, None), P(both), P("fsdp", None, "seq")
    in_specs = (rows, rows, rows, line, line, line, line, expert, expert, rows, rows, rows)
    out_specs = (rows, rows, rows, rows, line, line, line, line, expert, expert)
    return jax.shard_map(local, mesh=mesh, in_specs=in_specs, out_specs=out_specs, check_vma=False)
```

```python
import functools

import jax
import jax.numpy as jnp
from jax import lax
from jax.experimental import pallas as pl
from jax.experimental.pallas import tpu as pltpu
from jax.sharding import PartitionSpec as P


HD = 64
EPS = 1e-06
BF = jnp.bfloat16
F32 = jnp.float32
C0 = 0.7978845608028654
C1 = 0.044715


def mm(a, b):
    return jnp.dot(a, b, preferred_element_type=F32)


def mm_nt(a, b):
    return lax.dot_general(a, b, (((1,), (1,)), ((), ())), preferred_element_type=F32)


def mm_tn(a, b):
    return lax.dot_general(a, b, (((0,), (0,)), ((), ())), preferred_element_type=F32)


def kernel_call(body, outs, args, smem=0, scratch=()):
    vm = pl.BlockSpec(memory_space=pltpu.VMEM)
    sm = pl.BlockSpec(memory_space=pltpu.SMEM)
    return pl.pallas_call(
        body,
        out_shape=[jax.ShapeDtypeStruct(s, d) for s, d in outs],
        in_specs=[sm] * smem + [vm] * (len(args) - smem),
        out_specs=[vm] * len(outs),
        scratch_shapes=list(scratch),
    )(*args)


def exchange(chunks, axis, count, stride=1):
    got = [chunks[0]]
    for d in range(stride, count, stride):
        got.append(lax.ppermute(chunks[d // stride], axis, [(i, i ^ d) for i in range(count)]))
    return got


def swap(x, axis):
    return lax.all_to_all(x, axis, split_axis=0, concat_axis=0, tiled=True)


def after(x, *others):
    return lax.optimization_barrier((x, *others))[0]


def norm_stats(x):
    mean = jnp.mean(x, axis=-1, keepdims=True)
    centred = x - mean
    spread = jnp.mean(centred * centred, axis=-1, keepdims=True)
    return mean, centred, spread


def norm_parts(x):
    _, centred, spread = norm_stats(x)
    scale = lax.rsqrt(spread + EPS)
    return centred * scale, scale


def norm_back(hat, scale, gain, dy):
    dhat = dy * gain
    a = jnp.mean(dhat, axis=-1, keepdims=True)
    b = jnp.mean(dhat * hat, axis=-1, keepdims=True)
    return scale * (dhat - a - hat * b)


INFO = 8


def prepare_body(x_ref, cot_ref, info_ref, hat_ref, pack_ref):
    rows = x_ref.shape[0]
    mean, centred, spread = norm_stats(x_ref[...])
    scale = lax.rsqrt(spread + EPS)
    hat_ref[...] = (centred * scale).astype(BF)
    pack_ref[:rows, :] = cot_ref[...].astype(BF)
    lane = lax.broadcasted_iota(jnp.int32, info_ref.shape, 1)
    table = jnp.where(lane == 4, mean, jnp.where(lane == 5, scale, info_ref[...]))
    table = table.T[:INFO, :]
    high = table.astype(BF)
    rest = table - high.astype(F32)
    middle = rest.astype(BF)
    low = (rest - middle.astype(F32)).astype(BF)
    pack_ref[rows:, :] = jnp.zeros((pack_ref.shape[0] - rows, pack_ref.shape[1]), BF)
    span = table.shape[1]
    pack_ref[rows:, :span] = jnp.concatenate([high, middle], axis=0)
    pack_ref[rows:, span : 2 * span] = jnp.concatenate([low, jnp.zeros_like(low)], axis=0)


def table_body(experts, me_ref, *refs):
    blocks = refs[:-4]
    pos_ref, gate_ref, stat_ref, all_ref = refs[-4:]
    count = len(blocks)
    rows = blocks[0].shape[0] - 2 * INFO
    for d in range(count):
        first = blocks[d][rows:, :rows].astype(F32)
        second = blocks[d][rows:, rows : 2 * rows].astype(F32)
        values = first[:INFO, :] + first[INFO:, :] + second[:INFO, :]
        all_ref[me_ref[1] ^ d] = values
        wide = jnp.concatenate([values, jnp.zeros((rows - INFO, rows), F32)], axis=0)
        stat_ref[me_ref[1] ^ d] = wide.T
    flat = jnp.concatenate([all_ref[j] for j in range(count)], axis=1)
    tokens = flat.shape[1]
    first, second = flat[0:1, :], flat[1:2, :]
    left, right = flat[2:3, :], flat[3:4, :]
    top = jnp.maximum(left, right)
    left, right = jnp.exp(left - top), jnp.exp(right - top)
    total = left + right
    left, right = left / total, right / total
    label = lax.broadcasted_iota(jnp.int32, (experts, tokens), 0).astype(F32)
    is_first, is_second = label == first, label == second
    hit = is_first | is_second
    earlier = lax.broadcasted_iota(jnp.int32, (tokens, tokens), 0) < lax.broadcasted_iota(
        jnp.int32, (tokens, tokens), 1
    )
    rank = mm(jnp.where(hit, 1.0, 0.0).astype(BF), jnp.where(earlier, 1.0, 0.0).astype(BF))
    pos_ref[...] = jnp.where(hit, rank, -1.0)
    gate_ref[...] = jnp.where(is_first, left, 0.0) + jnp.where(is_second, right, 0.0)


def selection(pos_row, slots):
    tokens = pos_row.shape[1]
    slot = lax.broadcasted_iota(jnp.int32, (slots, tokens), 0).astype(F32)
    return slot == pos_row


def one_hot(pos_row, slots):
    return jnp.where(selection(pos_row, slots), 1.0, 0.0).astype(BF)


def dispatch_grad_body(experts, count, me_ref, pos_ref, gate_ref, *refs):
    blocks = refs[:count]
    out_ref, tok_ref = refs[count:]
    rows = blocks[0].shape[0] - 2 * INFO
    slots = out_ref.shape[1]
    for d in range(count):
        start = pl.multiple_of((me_ref[1] ^ d) * rows, rows)
        tok_ref[pl.ds(start, rows), :] = blocks[d][:rows, :]

    def step(e, carry):
        chosen = selection(pos_ref[pl.ds(e, 1), :], slots)
        pick = jnp.where(chosen, 1.0, 0.0).astype(BF)
        gate = jnp.sum(jnp.where(chosen, gate_ref[pl.ds(e, 1), :], 0.0), axis=1, keepdims=True)
        out_ref[e] = (mm(pick, tok_ref[...]) * gate).astype(BF)
        return carry

    lax.fori_loop(0, experts, step, 0)


def attention_forward_body(heads, me_ref, gains_ref, w_ref, *refs):
    blocks = refs[:-5]
    hat_ref, a_ref, qkv_ref, out_ref, lse_ref = refs[-5:]
    rows = blocks[0].shape[0]
    group = heads * HD
    for d in range(len(blocks)):
        start = pl.multiple_of((me_ref[1] ^ d) * rows, rows)
        hat_ref[pl.ds(start, rows), :] = blocks[d][...]
        a_ref[pl.ds(start, rows), :] = (
            blocks[d][...].astype(F32) * gains_ref[0:1, :] + gains_ref[1:2, :]
        ).astype(BF)
    qkv_ref[...] = mm(a_ref[...], w_ref[...]).astype(BF)
    for h in range(heads):
        q = qkv_ref[:, h * HD : (h + 1) * HD]
        k = qkv_ref[:, group + h * HD : group + (h + 1) * HD]
        v = qkv_ref[:, 2 * group + h * HD : 2 * group + (h + 1) * HD]
        scores = mm_nt(q, k) * HD ** (-0.5)
        top = jnp.max(scores, axis=-1, keepdims=True)
        weights = jnp.exp(scores - top)
        total = jnp.sum(weights, axis=-1, keepdims=True)
        probs = (weights / total).astype(BF)
        out_ref[:, h * HD : (h + 1) * HD] = mm(probs, v).astype(BF)
        lse_ref[:, h : h + 1] = top + jnp.log(total)


def attention_backward_body(heads, *refs):
    me_ref, own_ref = refs[:2]
    got = refs[2:-14]
    qkv_ref, lse_ref, w_ref, hat_ref, stat_ref, gains_ref, res_ref = refs[-14:-7]
    gqkv_ref, sums_ref, keep_ref = refs[-7:-4]
    send = refs[-4:-1]
    part_ref = refs[-1]
    group = heads * HD
    scale = HD ** (-0.5)
    grad_heads = own_ref[...]
    for ref in got:
        grad_heads = grad_heads + ref[...].astype(F32)
    grad_heads = grad_heads.astype(BF)
    for h in range(heads):
        q = qkv_ref[:, h * HD : (h + 1) * HD]
        k = qkv_ref[:, group + h * HD : group + (h + 1) * HD]
        v = qkv_ref[:, 2 * group + h * HD : 2 * group + (h + 1) * HD]
        g = grad_heads[:, h * HD : (h + 1) * HD]
        probs = jnp.exp(mm_nt(q, k) * scale - lse_ref[:, h : h + 1])
        grad_p = mm_nt(g, v)
        dots = jnp.sum(probs * grad_p, axis=-1, keepdims=True)
        grad_s = (probs * (grad_p - dots) * scale).astype(BF)
        gqkv_ref[:, h * HD : (h + 1) * HD] = mm(grad_s, k).astype(BF)
        gqkv_ref[:, group + h * HD : group + (h + 1) * HD] = mm_tn(grad_s, q).astype(BF)
        gqkv_ref[:, 2 * group + h * HD : 2 * group + (h + 1) * HD] = mm_tn(
            probs.astype(BF), g
        ).astype(BF)
    parts, rows, width = part_ref.shape
    part_ref[...] = mm_nt(gqkv_ref[...], w_ref[...]).reshape(parts, rows, width)
    sums_ref[...] = jnp.zeros(sums_ref.shape, F32)
    for j in range(parts):
        dy = part_ref[j]
        hat = hat_ref[j * rows : (j + 1) * rows, :].astype(F32)
        sums_ref[0:1, :] += jnp.sum(dy * hat, axis=0, keepdims=True)
        sums_ref[1:2, :] += jnp.sum(dy, axis=0, keepdims=True)
        part_ref[j] = res_ref[j] + norm_back(hat, stat_ref[j][:, 5:6], gains_ref[0:1, :], dy)
    spread_parts(me_ref[1], part_ref, keep_ref, send)


def spread_parts(me, part_ref, own_ref, send):
    own_ref[...] = part_ref[me]
    for d in range(1, part_ref.shape[0]):
        send[d - 1][...] = part_ref[me ^ d].astype(BF)


def split_pairs(me, temp_ref, keep_ref, send_ref, rows):
    odd = me & 1
    for q in range(keep_ref.shape[0]):
        keep_ref[q, :rows, :] = temp_ref[2 * q + odd]
        send_ref[q, :rows, :] = temp_ref[2 * q + 1 - odd].astype(BF)


def weight_grad_body(me_ref, a_ref, gqkv_ref, one_ref, two_ref, keep_ref, send_ref, temp_ref, line_ref):
    count, rows, width = temp_ref.shape
    temp_ref[...] = mm_tn(a_ref[...], gqkv_ref[...]).reshape(count, rows, width)
    split_pairs(me_ref[0], temp_ref, keep_ref, send_ref, rows)
    line_ref[...] = jnp.zeros(line_ref.shape, F32)
    for f in range(count):
        for k in range(4):
            source = one_ref if k < 2 else two_ref
            line_ref[f, 0:1, k * rows : (k + 1) * rows] = source[
                k % 2 : k % 2 + 1, f * rows : (f + 1) * rows
            ]
    odd = me_ref[0] & 1
    for q in range(keep_ref.shape[0]):
        keep_ref[q, rows:, :] = line_ref[2 * q + odd]
        send_ref[q, rows:, :] = line_ref[2 * q + 1 - odd].astype(BF)


def proj_grad_body(count, me_ref, mix_ref, *refs):
    heads = refs[:count]
    keep_ref, send_ref, full_ref, temp_ref = refs[count:]
    width = heads[0].shape[1]
    for d in range(count):
        start = pl.multiple_of((me_ref[1] ^ d) * width, width)
        full_ref[pl.ds(start, width), :] = mm_tn(heads[d][...], mix_ref[...])
    temp_ref[...] = full_ref[...].reshape(temp_ref.shape)
    split_pairs(me_ref[0], temp_ref, keep_ref, send_ref, temp_ref.shape[1])


def pair_sum_body(me_ref, keep_ref, got_ref, *out_refs):
    pair = me_ref[0] >> 1
    for k, ref in enumerate(out_refs):
        ref[...] = (keep_ref[pair ^ k] + got_ref[pair ^ k].astype(F32)).astype(BF)


def total_of(refs):
    total = refs[0][...].astype(F32)
    for ref in refs[1:]:
        total = total + ref[...].astype(F32)
    return total


def last_sum_body(blocks, rows, count, me_ref, *refs):
    total, proj = total_of(refs[:count]), total_of(refs[count : 2 * count])
    sends, out_ref = refs[2 * count : -1], refs[-1]
    each, cols = rows // blocks, total.shape[1]
    out_ref[...] = jnp.zeros(out_ref.shape, BF)
    for s in range(blocks):
        out_ref[s, :each, :cols] = total[s * each : (s + 1) * each, :].astype(BF)
        out_ref[s, :each, cols:] = proj[s * each : (s + 1) * each, :].astype(BF)
        for k in range(4):
            start = k * rows + s * each
            out_ref[s, each : each + 1, k * each : (k + 1) * each] = total[
                rows : rows + 1, start : start + each
            ].astype(BF)
    for d, ref in enumerate(sends):
        ref[...] = out_ref[me_ref[1] ^ d]


def last_body(each, group, me_ref, *refs):
    out_ref, proj_ref, line_ref, parts_ref = refs[-4:]
    blocks = parts_ref.shape[0]
    for d in range(blocks):
        parts_ref[me_ref[1] ^ d] = refs[d][...]
    width = blocks * group
    line = jnp.zeros(line_ref.shape, F32)
    proj = jnp.zeros(proj_ref.shape, F32)
    for s in range(blocks):
        part = parts_ref[s].astype(F32)
        proj = proj + part[:each, 3 * group :]
        for p in range(3):
            start = p * width + s * group
            out_ref[:, start : start + group] = part[:each, p * group : (p + 1) * group]
        line = line + part[each : each + 1, : line_ref.shape[1]]
    line_ref[...] = line
    proj_ref[...] = proj


def project_body(count, me_ref, pos_ref, hat_ref, stat_ref, x_ref, gains_ref, proj_ref, *refs):
    heads = refs[:count]
    res_ref, own_ref = refs[count : count + 2]
    out_refs = refs[count + 2 : -2]
    acc_ref, ffn_ref = refs[-2:]
    rows = x_ref.shape[0]
    group = heads[0].shape[1]
    for d in range(count):
        start = pl.multiple_of((me_ref[1] ^ d) * group, group)
        piece = mm(heads[d][...], proj_ref[pl.ds(start, group), :])
        acc_ref[...] = piece if d == 0 else acc_ref[...] + piece
    for j in range(count):
        stat = stat_ref[j]
        x = hat_ref[j * rows : (j + 1) * rows, :].astype(F32) / stat[:, 5:6] + stat[:, 4:5]
        x = jnp.where(me_ref[1] == j, x_ref[...], x)
        res_ref[j] = x + acc_ref[j * rows : (j + 1) * rows, :]
        hat, _ = norm_parts(res_ref[j])
        ffn_ref[j * rows : (j + 1) * rows, :] = (
            hat * gains_ref[2:3, :] + gains_ref[3:4, :]
        ).astype(BF)
    own_ref[...] = res_ref[me_ref[1]]
    for d, out_ref in enumerate(out_refs):
        pick = one_hot(pos_ref[pl.ds(me_ref[0] ^ d, 1), :], out_ref.shape[0])
        out_ref[...] = mm(pick, ffn_ref[...]).astype(BF)


def combine_grad_body(experts, me_ref, pos_ref, res_ref, cot_ref, gains_ref, proj_ref, *refs):
    back = refs[:experts]
    dx_ref, mix_ref, sums_ref, keep_ref = refs[experts : experts + 4]
    send = refs[experts + 4 : -1]
    part_ref = refs[-1]
    slots = back[0].shape[0]
    parts, rows, width = part_ref.shape
    for d in range(experts):
        pick = one_hot(pos_ref[pl.ds(me_ref[0] ^ d, 1), :], slots)
        piece = mm_tn(pick, back[d][...]).reshape(parts, rows, width)
        part_ref[...] = piece if d == 0 else part_ref[...] + piece
    sums_ref[...] = jnp.zeros(sums_ref.shape, F32)
    for j in range(parts):
        dy = part_ref[j]
        hat, scale = norm_parts(res_ref[j])
        sums_ref[0:1, :] += jnp.sum(dy * hat, axis=0, keepdims=True)
        sums_ref[1:2, :] += jnp.sum(dy, axis=0, keepdims=True)
        dx = norm_back(hat, scale, gains_ref[2:3, :], dy)
        dx = dx + jnp.where(me_ref[1] == j, cot_ref[...], 0.0)
        dx_ref[j] = dx
        mix_ref[j * rows : (j + 1) * rows, :] = dx.astype(BF)
    group = keep_ref.shape[1]
    for d in range(parts):
        start = pl.multiple_of((me_ref[1] ^ d) * group, group)
        piece = mm_nt(mix_ref[...], proj_ref[pl.ds(start, group), :])
        if d == 0:
            keep_ref[...] = piece
        else:
            send[d - 1][...] = piece.astype(BF)


def combine_out_body(experts, me_ref, pos_ref, gate_ref, back_ref, res_ref, own_ref, *refs):
    send, part_ref = refs[:-1], refs[-1]
    slots = back_ref.shape[1]
    parts, rows, width = part_ref.shape
    part_ref[...] = jnp.zeros(part_ref.shape, F32)

    def step(e, carry):
        chosen = selection(pos_ref[pl.ds(e, 1), :], slots)
        gate = jnp.where(chosen, gate_ref[pl.ds(e, 1), :], 0.0)
        high = gate.astype(BF)
        low = (gate - high.astype(F32)).astype(BF)
        piece = mm_tn(high, back_ref[e]) + mm_tn(low, back_ref[e])
        part_ref[...] += piece.reshape(parts, rows, width)
        return carry

    lax.fori_loop(0, experts, step, 0)
    spread_parts(me_ref[1], part_ref, own_ref, send)
    own_ref[...] += res_ref[...]


def hidden_grad_body(per, me_ref, g_ref, down_ref, *out_refs):
    rows = g_ref.shape[1]
    for g, out_ref in enumerate(out_refs):
        for i in range(per):
            out_ref[i * rows : (i + 1) * rows, :] = mm(
                g_ref[me_ref[0] ^ (g * per + i)], down_ref[...]
            )


def expert_body(count, *refs):
    rows_refs = refs[:count]
    gh_ref, up_ref = refs[count : count + 2]
    gr_refs = refs[count + 2 : 2 * count + 2]
    hid_ref, gp_ref, pre_ref = refs[2 * count + 2 :]
    rows = rows_refs[0].shape[0]
    for i in range(count):
        pre_ref[i * rows : (i + 1) * rows, :] = mm(rows_refs[i][...], up_ref[...])
    tile = 32

    def step(j, carry):
        at = pl.ds(pl.multiple_of(j * tile, tile), tile)
        u = pre_ref[at, :]
        sq = u * u
        t = jnp.tanh(C0 * (u + C1 * (sq * u)))
        half = 0.5 * (1.0 + t)
        hid_ref[at, :] = (u * half).astype(BF)
        slope = half + 0.5 * u * (1.0 - t * t) * (C0 * (1.0 + 3.0 * C1 * sq))
        gp_ref[at, :] = (gh_ref[at, :] * slope).astype(BF)
        return carry

    lax.fori_loop(0, count * rows // tile, step, 0)
    for i in range(count):
        gr_refs[i][...] = mm_nt(gp_ref[i * rows : (i + 1) * rows, :], up_ref[...]).astype(BF)


def expert_out_body(per, me_ref, down_ref, *refs):
    hids, out_ref = refs[:-1], refs[-1]
    rows = out_ref.shape[1]
    for g, hid_ref in enumerate(hids):
        for i in range(per):
            out_ref[me_ref[0] ^ (g * per + i)] = mm_nt(
                hid_ref[i * rows : (i + 1) * rows, :], down_ref[...]
            ).astype(BF)


def grad_up_body(count, *refs):
    lefts, rights, out_ref, temp_ref = refs[: -2 - count], refs[-2 - count : -2], refs[-2], refs[-1]
    rows = lefts[0].shape[0]
    per = len(lefts) // count
    for g in range(count):
        for i in range(per):
            temp_ref[i * rows : (i + 1) * rows, :] = lefts[g * per + i][...]
        piece = mm_tn(temp_ref[...], rights[g][...])
        out_ref[0] = piece if g == 0 else out_ref[0] + piece


def grad_down_body(count, me_ref, left_ref, *refs):
    rights, out_ref, temp_ref = refs[:count], refs[count], refs[count + 1]
    rows = left_ref.shape[1]
    per = left_ref.shape[0] // count
    for g in range(count):
        for i in range(per):
            temp_ref[i * rows : (i + 1) * rows, :] = left_ref[me_ref[0] ^ (g * per + i)]
        piece = mm_tn(temp_ref[...], rights[g][...])
        out_ref[0] = piece if g == 0 else out_ref[0] + piece


def local(
    inputs,
    qkv_weight,
    proj_weight,
    first_gain,
    first_shift,
    second_gain,
    second_shift,
    expert_up,
    expert_down,
    gate_logits,
    routes,
    cotangent,
):
    tok, width = inputs.shape
    ns = lax.axis_size("seq")
    nf = lax.axis_size("fsdp")
    group = width // ns
    heads = group // HD
    length = tok * ns
    slots = ns * (4 * tok // nf)
    wrows = qkv_weight.shape[0]
    cols = 3 * group
    hidden = expert_up.shape[2]
    me = jnp.stack([lax.axis_index("fsdp"), lax.axis_index("seq")]).astype(jnp.int32)
    groups = 4
    per = nf // groups
    bf_block = ((tok, width), BF)

    by_group = qkv_weight.reshape(wrows, 3, ns, group).transpose(2, 0, 1, 3).reshape(ns, wrows, cols)
    packed = jnp.concatenate(
        [by_group, jnp.broadcast_to(proj_weight[None], (ns, wrows, width))], axis=2
    )
    gain_row = jnp.concatenate([first_gain, first_shift, second_gain, second_shift])
    gain_row = jnp.pad(gain_row, (0, cols + width - gain_row.shape[0]))
    packed = jnp.concatenate(
        [packed, jnp.broadcast_to(gain_row[None, None, :], (ns, 1, cols + width))], axis=1
    )
    packed = swap(packed, "seq")
    info = jnp.concatenate([routes.astype(F32), gate_logits], axis=1)
    info = jnp.pad(info, ((0, 0), (0, tok - info.shape[1])))
    hat_own, cot_pack = kernel_call(
        prepare_body, [bf_block, ((tok + 2 * INFO, width), BF)], (inputs, cotangent, info)
    )
    cot_blocks = exchange([cot_pack] * ns, "seq", ns)
    first = lax.all_gather(packed[:, :, :cols], "fsdp", axis=0, tiled=True)
    hat_own, proj_rows, me_late, first = lax.optimization_barrier(
        (hat_own, packed[:, :wrows, cols:].reshape(ns * wrows, width), me, first)
    )
    hat_blocks = exchange([hat_own] * ns, "seq", ns)
    qkv_w = first[:, :wrows].reshape(width, cols)
    gains = (
        first[:, wrows, : 4 * wrows]
        .reshape(nf * ns, 4, wrows)
        .transpose(1, 0, 2)
        .reshape(4, width)
        .astype(F32)
    )
    proj = swap(jnp.broadcast_to(proj_rows[None], (nf, ns * wrows, width)), "fsdp")
    proj = proj.reshape(width, width)

    pos, gate, stats = kernel_call(
        functools.partial(table_body, nf),
        [((nf, length), F32), ((nf, length), F32), ((ns, tok, tok), F32)],
        (me_late, *cot_blocks),
        smem=1,
        scratch=[pltpu.VMEM((ns, INFO, tok), F32)],
    )
    (grad_sent,) = kernel_call(
        functools.partial(dispatch_grad_body, nf, ns),
        [((nf, slots, width), BF)],
        (me, pos, gate, *cot_blocks),
        smem=1,
        scratch=[pltpu.VMEM((length, width), BF)],
    )
    grad_in = swap(grad_sent, "fsdp")
    up, down = expert_up[0], expert_down[0]

    hat, attn_in, qkv, heads_s, lse = kernel_call(
        functools.partial(attention_forward_body, heads),
        [
            ((length, width), BF),
            ((length, width), BF),
            ((length, cols), BF),
            ((length, group), BF),
            ((length, 128), F32),
        ],
        (me, gains, qkv_w, *hat_blocks),
        smem=1,
    )
    heads_all = exchange([heads_s] * ns, "seq", ns)
    grad_hidden = kernel_call(
        functools.partial(hidden_grad_body, per),
        [((per * slots, hidden), F32)] * groups,
        (me, grad_in, down),
        smem=1,
    )
    res_all, residual, *sent = kernel_call(
        functools.partial(project_body, ns),
        [((ns, tok, width), F32), ((tok, width), F32)] + [((slots, width), BF)] * nf,
        (me, pos, hat, stats, inputs, gains, proj, *heads_all),
        smem=1,
        scratch=[pltpu.VMEM((length, width), F32), pltpu.VMEM((length, width), BF)],
    )
    rows_in = exchange(sent, "fsdp", nf)
    grad_rows, hid, grad_pre = [], [], []
    for g in range(groups):
        res = kernel_call(
            functools.partial(expert_body, per),
            [((slots, width), BF)] * per + [((per * slots, hidden), BF)] * 2,
            (*rows_in[g * per : (g + 1) * per], grad_hidden[g], up),
            scratch=[pltpu.VMEM((per * slots, hidden), F32)],
        )
        grad_rows += res[:per]
        hid.append(res[per])
        grad_pre.append(res[per + 1])
    grad_back = exchange(grad_rows, "fsdp", nf)
    (expert_out,) = kernel_call(
        functools.partial(expert_out_body, per),
        [((nf, slots, width), BF)],
        (me, down, *hid),
        smem=1,
    )
    temp = [pltpu.VMEM((per * slots, width), BF)]
    (grad_up,) = kernel_call(
        functools.partial(grad_up_body, groups),
        [((1, width, hidden), F32)],
        (*rows_in, *grad_pre),
        scratch=temp,
    )
    (grad_down,) = kernel_call(
        functools.partial(grad_down_body, groups),
        [((1, width, hidden), F32)],
        (me, grad_in, *hid),
        smem=1,
        scratch=temp,
    )

    image = [pltpu.VMEM((ns, tok, width), F32)]
    share = [((tok, width), F32)] + [bf_block] * (ns - 1)
    grad_res, mix, sums_two, gh_own, *gh_sent = kernel_call(
        functools.partial(combine_grad_body, nf),
        [
            ((ns, tok, width), F32),
            ((length, width), BF),
            ((2, width), F32),
            ((length, group), F32),
        ]
        + [((length, group), BF)] * (ns - 1),
        (me, pos, res_all, cotangent, gains, proj, *grad_back),
        smem=1,
        scratch=image,
    )
    out_back = swap(after(expert_out, gh_own), "fsdp")
    gh_got = exchange([None] + gh_sent, "seq", ns)[1:]
    grad_qkv, sums_one, grad_own, *grad_share = kernel_call(
        functools.partial(attention_backward_body, heads),
        [((length, cols), BF), ((2, width), F32)] + share,
        (me, gh_own, *gh_got, qkv, lse, qkv_w, hat, stats, gains, grad_res),
        smem=1,
        scratch=image,
    )
    grad_inputs = grad_own
    for piece in exchange([None] + grad_share, "seq", ns)[1:]:
        grad_inputs = grad_inputs + piece.astype(F32)
    wide = ns * wrows
    half = nf // 2

    def over_chips(keep, sent):
        got = lax.ppermute(sent, "fsdp", [(i, i ^ 1) for i in range(nf)])
        both = kernel_call(pair_sum_body, [(keep.shape[1:], BF)] * half, (me, keep, got), smem=1)
        return exchange(both, "fsdp", nf, stride=2)

    keep_p, send_p = kernel_call(
        functools.partial(proj_grad_body, ns),
        [((half, wide, width), F32), ((half, wide, width), BF)],
        (me, mix, *heads_all),
        smem=1,
        scratch=[pltpu.VMEM((width, width), F32), pltpu.VMEM((nf, wide, width), F32)],
    )
    parts_p = over_chips(keep_p, send_p)
    keep_q, send_q = kernel_call(
        weight_grad_body,
        [((half, wide + 8, cols), F32), ((half, wide + 8, cols), BF)],
        (me, attn_in, grad_qkv, sums_one, sums_two),
        smem=1,
        scratch=[pltpu.VMEM((nf, wide, cols), F32), pltpu.VMEM((nf, 8, cols), F32)],
    )
    parts_q = over_chips(keep_q, send_q)
    last = kernel_call(
        functools.partial(last_sum_body, ns, wide, half),
        [((wrows + 8, cols + width), BF)] * ns,
        (me, *parts_q, *parts_p),
        smem=1,
        scratch=[pltpu.VMEM((ns, wrows + 8, cols + width), BF)],
    )
    last = exchange(last, "seq", ns)
    grad_qkv_weight, grad_proj, line = kernel_call(
        functools.partial(last_body, wrows, group),
        [((wrows, 3 * width), F32), ((wrows, width), F32), ((1, 128), F32)],
        (me, *last),
        smem=1,
        scratch=[pltpu.VMEM((ns, wrows + 8, cols + width), BF)],
    )
    tiny = line[0, : 4 * wrows].reshape(4, wrows)
    output, *out_share = kernel_call(
        functools.partial(combine_out_body, nf),
        share,
        (me, pos, gate, out_back, residual),
        smem=1,
        scratch=image,
    )
    for piece in exchange([None] + out_share, "seq", ns)[1:]:
        output = output + piece.astype(F32)

    return (
        output,
        grad_inputs,
        grad_qkv_weight,
        grad_proj,
        tiny[0],
        tiny[1],
        tiny[2],
        tiny[3],
        grad_up,
        grad_down,
    )


def solution(mesh):
    both = ("fsdp", "seq")
    rows, line, expert = P(both, None), P(both), P("fsdp", None, "seq")
    in_specs = (rows, rows, rows, line, line, line, line, expert, expert, rows, rows, rows)
    out_specs = (rows, rows, rows, rows, line, line, line, line, expert, expert)
    return jax.shard_map(local, mesh=mesh, in_specs=in_specs, out_specs=out_specs, check_vma=False)
```

```python
import functools

import jax
import jax.numpy as jnp
from jax import lax
from jax.experimental import pallas as pl
from jax.experimental.pallas import tpu as pltpu
from jax.sharding import PartitionSpec as P


HD = 64
EPS = 1e-06
BF = jnp.bfloat16
F32 = jnp.float32
C0 = 0.7978845608028654
C1 = 0.044715


def mm(a, b):
    return jnp.dot(a, b, preferred_element_type=F32)


def mm_nt(a, b):
    return lax.dot_general(a, b, (((1,), (1,)), ((), ())), preferred_element_type=F32)


def mm_tn(a, b):
    return lax.dot_general(a, b, (((0,), (0,)), ((), ())), preferred_element_type=F32)


def kernel_call(body, outs, args, smem=0, scratch=()):
    vm = pl.BlockSpec(memory_space=pltpu.VMEM)
    sm = pl.BlockSpec(memory_space=pltpu.SMEM)
    return pl.pallas_call(
        body,
        out_shape=[jax.ShapeDtypeStruct(s, d) for s, d in outs],
        in_specs=[sm] * smem + [vm] * (len(args) - smem),
        out_specs=[vm] * len(outs),
        scratch_shapes=list(scratch),
    )(*args)


def exchange(chunks, axis, count, stride=1):
    got = [chunks[0]]
    for d in range(stride, count, stride):
        got.append(lax.ppermute(chunks[d // stride], axis, [(i, i ^ d) for i in range(count)]))
    return got


def swap(x, axis):
    return lax.all_to_all(x, axis, split_axis=0, concat_axis=0, tiled=True)


def after(x, *others):
    return lax.optimization_barrier((x, *others))[0]


def norm_stats(x):
    mean = jnp.mean(x, axis=-1, keepdims=True)
    centred = x - mean
    spread = jnp.mean(centred * centred, axis=-1, keepdims=True)
    return mean, centred, spread


def norm_parts(x):
    _, centred, spread = norm_stats(x)
    scale = lax.rsqrt(spread + EPS)
    return centred * scale, scale


def norm_back(hat, scale, gain, dy):
    dhat = dy * gain
    a = jnp.mean(dhat, axis=-1, keepdims=True)
    b = jnp.mean(dhat * hat, axis=-1, keepdims=True)
    return scale * (dhat - a - hat * b)


INFO = 8


def prepare_body(x_ref, cot_ref, info_ref, hat_ref, pack_ref):
    rows = x_ref.shape[0]
    mean, centred, spread = norm_stats(x_ref[...])
    scale = lax.rsqrt(spread + EPS)
    hat_ref[...] = (centred * scale).astype(BF)
    pack_ref[:rows, :] = cot_ref[...].astype(BF)
    lane = lax.broadcasted_iota(jnp.int32, info_ref.shape, 1)
    table = jnp.where(lane == 4, mean, jnp.where(lane == 5, scale, info_ref[...]))
    table = table.T[:INFO, :]
    high = table.astype(BF)
    rest = table - high.astype(F32)
    middle = rest.astype(BF)
    low = (rest - middle.astype(F32)).astype(BF)
    pack_ref[rows:, :] = jnp.zeros((pack_ref.shape[0] - rows, pack_ref.shape[1]), BF)
    span = table.shape[1]
    pack_ref[rows:, :span] = jnp.concatenate([high, middle], axis=0)
    pack_ref[rows:, span : 2 * span] = jnp.concatenate([low, jnp.zeros_like(low)], axis=0)


def table_body(experts, capacity, me_ref, *refs):
    blocks = refs[:-3]
    table_ref, stat_ref, all_ref = refs[-3:]
    count = len(blocks)
    rows = blocks[0].shape[0] - 2 * INFO
    for d in range(count):
        first = blocks[d][rows:, :rows].astype(F32)
        second = blocks[d][rows:, rows : 2 * rows].astype(F32)
        values = first[:INFO, :] + first[INFO:, :] + second[:INFO, :]
        all_ref[me_ref[1] ^ d] = values
        wide = jnp.concatenate([values, jnp.zeros((rows - INFO, rows), F32)], axis=0)
        stat_ref[me_ref[1] ^ d] = wide.T
    flat = jnp.concatenate([all_ref[j] for j in range(count)], axis=1)
    first, second = flat[0:1, :], flat[1:2, :]
    left, right = flat[2:3, :], flat[3:4, :]
    top = jnp.maximum(left, right)
    left, right = jnp.exp(left - top), jnp.exp(right - top)
    total = left + right
    earlier = lax.broadcasted_iota(jnp.int32, (rows, rows), 0) < lax.broadcasted_iota(
        jnp.int32, (rows, rows), 1
    )
    earlier = jnp.where(earlier, 1.0, 0.0).astype(BF)
    label = lax.broadcasted_iota(jnp.int32, (experts, flat.shape[1]), 0).astype(F32)
    is_first, is_second = label == first, label == second
    hit = jnp.where(is_first | is_second, 1.0, 0.0).astype(BF)
    rank = jnp.concatenate(
        [mm(hit[:, j * rows : (j + 1) * rows], earlier) for j in range(count)], axis=1
    )
    for k, (route, chosen) in enumerate(((first, is_first), (second, is_second))):
        place = jnp.sum(jnp.where(chosen, rank, 0.0), axis=0, keepdims=True)
        turned = (route.astype(jnp.int32) ^ me_ref[0]).astype(F32)
        table_ref[k : k + 1, :] = turned * capacity + place
        table_ref[2 + k : 3 + k, :] = route * capacity + place
    table_ref[4:5, :] = left / total
    table_ref[5:6, :] = right / total
    table_ref[6:8, :] = jnp.zeros((2, flat.shape[1]), F32)


def matches(table_ref, row, block, rows, slots):
    slot = lax.broadcasted_iota(jnp.int32, (slots, rows), 0).astype(F32)
    lanes = slice(block * rows, (block + 1) * rows)
    return [slot == table_ref[row + k : row + k + 1, lanes] for k in range(2)]


def one_hot(table_ref, row, block, rows, slots):
    first, second = matches(table_ref, row, block, rows, slots)
    return jnp.where(first | second, 1.0, 0.0).astype(BF)


def gate_hot(table_ref, row, block, rows, slots):
    first, second = matches(table_ref, row, block, rows, slots)
    lanes = slice(block * rows, (block + 1) * rows)
    return jnp.where(first, table_ref[4:5, lanes], 0.0) + jnp.where(
        second, table_ref[5:6, lanes], 0.0
    )


def dispatch_grad_body(count, me_ref, table_ref, *refs):
    blocks = refs[:count]
    out_ref, tok_ref = refs[count:]
    rows = blocks[0].shape[0] - 2 * INFO
    experts, slots, width = out_ref.shape
    capacity = slots // count
    for d in range(count):
        tok_ref[me_ref[1] ^ d] = blocks[d][:rows, :]
    for j in range(count):
        pick = one_hot(table_ref, 2, j, rows, experts * capacity)
        gate = gate_hot(table_ref, 2, j, rows, experts * capacity)
        gate = jnp.sum(gate, axis=1, keepdims=True)
        value = (mm(pick, tok_ref[j]) * gate).reshape(experts, capacity, width)
        out_ref[:, j * capacity : (j + 1) * capacity, :] = value.astype(BF)


def attention_forward_body(heads, me_ref, gains_ref, w_ref, *refs):
    blocks = refs[:-5]
    hat_ref, a_ref, qkv_ref, out_ref, lse_ref = refs[-5:]
    rows = blocks[0].shape[0]
    group = heads * HD
    for d in range(len(blocks)):
        start = pl.multiple_of((me_ref[1] ^ d) * rows, rows)
        hat_ref[pl.ds(start, rows), :] = blocks[d][...]
        a_ref[pl.ds(start, rows), :] = (
            blocks[d][...].astype(F32) * gains_ref[0:1, :] + gains_ref[1:2, :]
        ).astype(BF)
    qkv_ref[...] = mm(a_ref[...], w_ref[...]).astype(BF)
    for h in range(heads):
        q = qkv_ref[:, h * HD : (h + 1) * HD]
        k = qkv_ref[:, group + h * HD : group + (h + 1) * HD]
        v = qkv_ref[:, 2 * group + h * HD : 2 * group + (h + 1) * HD]
        scores = mm_nt(q, k) * HD ** (-0.5)
        top = jnp.max(scores, axis=-1, keepdims=True)
        weights = jnp.exp(scores - top)
        total = jnp.sum(weights, axis=-1, keepdims=True)
        probs = (weights / total).astype(BF)
        out_ref[:, h * HD : (h + 1) * HD] = mm(probs, v).astype(BF)
        lse_ref[:, h : h + 1] = top + jnp.log(total)


def attention_backward_body(heads, *refs):
    me_ref, own_ref = refs[:2]
    got = refs[2:-14]
    qkv_ref, lse_ref, w_ref, hat_ref, stat_ref, gains_ref, res_ref = refs[-14:-7]
    gqkv_ref, sums_ref, keep_ref = refs[-7:-4]
    send = refs[-4:-1]
    part_ref = refs[-1]
    group = heads * HD
    scale = HD ** (-0.5)
    grad_heads = own_ref[...]
    for ref in got:
        grad_heads = grad_heads + ref[...].astype(F32)
    grad_heads = grad_heads.astype(BF)
    for h in range(heads):
        q = qkv_ref[:, h * HD : (h + 1) * HD]
        k = qkv_ref[:, group + h * HD : group + (h + 1) * HD]
        v = qkv_ref[:, 2 * group + h * HD : 2 * group + (h + 1) * HD]
        g = grad_heads[:, h * HD : (h + 1) * HD]
        probs = jnp.exp(mm_nt(q, k) * scale - lse_ref[:, h : h + 1])
        grad_p = mm_nt(g, v)
        dots = jnp.sum(probs * grad_p, axis=-1, keepdims=True)
        grad_s = (probs * (grad_p - dots) * scale).astype(BF)
        gqkv_ref[:, h * HD : (h + 1) * HD] = mm(grad_s, k).astype(BF)
        gqkv_ref[:, group + h * HD : group + (h + 1) * HD] = mm_tn(grad_s, q).astype(BF)
        gqkv_ref[:, 2 * group + h * HD : 2 * group + (h + 1) * HD] = mm_tn(
            probs.astype(BF), g
        ).astype(BF)
    parts, rows, width = part_ref.shape
    part_ref[...] = mm_nt(gqkv_ref[...], w_ref[...]).reshape(parts, rows, width)
    sums_ref[...] = jnp.zeros(sums_ref.shape, F32)
    for j in range(parts):
        dy = part_ref[j]
        hat = hat_ref[j * rows : (j + 1) * rows, :].astype(F32)
        sums_ref[0:1, :] += jnp.sum(dy * hat, axis=0, keepdims=True)
        sums_ref[1:2, :] += jnp.sum(dy, axis=0, keepdims=True)
        part_ref[j] = res_ref[j] + norm_back(hat, stat_ref[j][:, 5:6], gains_ref[0:1, :], dy)
    spread_parts(me_ref[1], part_ref, keep_ref, send)


def spread_parts(me, part_ref, own_ref, send):
    own_ref[...] = part_ref[me]
    for d in range(1, part_ref.shape[0]):
        send[d - 1][...] = part_ref[me ^ d].astype(BF)


def split_pairs(me, temp_ref, keep_ref, send_ref, rows):
    odd = me & 1
    for q in range(keep_ref.shape[0]):
        keep_ref[q, :rows, :] = temp_ref[2 * q + odd]
        send_ref[q, :rows, :] = temp_ref[2 * q + 1 - odd].astype(BF)


def weight_grad_body(me_ref, a_ref, gqkv_ref, one_ref, two_ref, keep_ref, send_ref, temp_ref, line_ref):
    count, rows, width = temp_ref.shape
    temp_ref[...] = mm_tn(a_ref[...], gqkv_ref[...]).reshape(count, rows, width)
    split_pairs(me_ref[0], temp_ref, keep_ref, send_ref, rows)
    line_ref[...] = jnp.zeros(line_ref.shape, F32)
    for f in range(count):
        for k in range(4):
            source = one_ref if k < 2 else two_ref
            line_ref[f, 0:1, k * rows : (k + 1) * rows] = source[
                k % 2 : k % 2 + 1, f * rows : (f + 1) * rows
            ]
    odd = me_ref[0] & 1
    for q in range(keep_ref.shape[0]):
        keep_ref[q, rows:, :] = line_ref[2 * q + odd]
        send_ref[q, rows:, :] = line_ref[2 * q + 1 - odd].astype(BF)


def proj_grad_body(count, me_ref, mix_ref, *refs):
    heads = refs[:count]
    keep_ref, send_ref, full_ref, temp_ref = refs[count:]
    width = heads[0].shape[1]
    for d in range(count):
        start = pl.multiple_of((me_ref[1] ^ d) * width, width)
        full_ref[pl.ds(start, width), :] = mm_tn(heads[d][...], mix_ref[...])
    temp_ref[...] = full_ref[...].reshape(temp_ref.shape)
    split_pairs(me_ref[0], temp_ref, keep_ref, send_ref, temp_ref.shape[1])


def pair_sum_body(me_ref, keep_ref, got_ref, *out_refs):
    pair = me_ref[0] >> 1
    for k, ref in enumerate(out_refs):
        ref[...] = (keep_ref[pair ^ k] + got_ref[pair ^ k].astype(F32)).astype(BF)


def total_of(refs):
    total = refs[0][...].astype(F32)
    for ref in refs[1:]:
        total = total + ref[...].astype(F32)
    return total


def last_sum_body(blocks, rows, count, me_ref, *refs):
    total, proj = total_of(refs[:count]), total_of(refs[count : 2 * count])
    sends, out_ref = refs[2 * count : -1], refs[-1]
    each, cols = rows // blocks, total.shape[1]
    out_ref[...] = jnp.zeros(out_ref.shape, BF)
    for s in range(blocks):
        out_ref[s, :each, :cols] = total[s * each : (s + 1) * each, :].astype(BF)
        out_ref[s, :each, cols:] = proj[s * each : (s + 1) * each, :].astype(BF)
        for k in range(4):
            start = k * rows + s * each
            out_ref[s, each : each + 1, k * each : (k + 1) * each] = total[
                rows : rows + 1, start : start + each
            ].astype(BF)
    for d, ref in enumerate(sends):
        ref[...] = out_ref[me_ref[1] ^ d]


def last_body(each, group, me_ref, *refs):
    out_ref, proj_ref, line_ref, parts_ref = refs[-4:]
    blocks = parts_ref.shape[0]
    for d in range(blocks):
        parts_ref[me_ref[1] ^ d] = refs[d][...]
    width = blocks * group
    line = jnp.zeros(line_ref.shape, F32)
    proj = jnp.zeros(proj_ref.shape, F32)
    for s in range(blocks):
        part = parts_ref[s].astype(F32)
        proj = proj + part[:each, 3 * group :]
        for p in range(3):
            start = p * width + s * group
            out_ref[:, start : start + group] = part[:each, p * group : (p + 1) * group]
        line = line + part[each : each + 1, : line_ref.shape[1]]
    line_ref[...] = line
    proj_ref[...] = proj


def project_body(count, peers, me_ref, table_ref, hat_ref, stat_ref, x_ref, gains_ref, *refs):
    heads, chunks = refs[:count], refs[count : count + peers]
    res_ref, own_ref, proj_ref = refs[count + peers : count + peers + 3]
    out_refs = refs[count + peers + 3 : -2]
    acc_ref, ffn_ref = refs[-2:]
    rows = x_ref.shape[0]
    span = chunks[0].shape[0]
    for d in range(peers):
        start = pl.multiple_of((me_ref[0] ^ d) * span, span)
        proj_ref[pl.ds(start, span), :] = chunks[d][...]
    group = heads[0].shape[1]
    for d in range(count):
        start = pl.multiple_of((me_ref[1] ^ d) * group, group)
        piece = mm(heads[d][...], proj_ref[pl.ds(start, group), :])
        acc_ref[...] = piece if d == 0 else acc_ref[...] + piece
    for j in range(count):
        stat = stat_ref[j]
        x = hat_ref[j * rows : (j + 1) * rows, :].astype(F32) / stat[:, 5:6] + stat[:, 4:5]
        x = jnp.where(me_ref[1] == j, x_ref[...], x)
        res_ref[j] = x + acc_ref[j * rows : (j + 1) * rows, :]
        hat, _ = norm_parts(res_ref[j])
        ffn_ref[j * rows : (j + 1) * rows, :] = (
            hat * gains_ref[2:3, :] + gains_ref[3:4, :]
        ).astype(BF)
    own_ref[...] = res_ref[me_ref[1]]
    capacity = out_refs[0].shape[0] // count
    for j in range(count):
        pick = one_hot(table_ref, 0, j, rows, len(out_refs) * capacity)
        value = mm(pick, ffn_ref[j * rows : (j + 1) * rows, :]).astype(BF)
        for d, out_ref in enumerate(out_refs):
            out_ref[j * capacity : (j + 1) * capacity, :] = value[
                d * capacity : (d + 1) * capacity, :
            ]


def combine_grad_body(experts, me_ref, table_ref, res_ref, cot_ref, gains_ref, proj_ref, *refs):
    back = refs[:experts]
    dx_ref, mix_ref, sums_ref, keep_ref = refs[experts : experts + 4]
    send = refs[experts + 4 : -2]
    part_ref, line_ref = refs[-2:]
    parts, rows, _ = part_ref.shape
    capacity = back[0].shape[0] // parts
    for j in range(parts):
        for d in range(experts):
            line_ref[j, d * capacity : (d + 1) * capacity, :] = back[d][
                j * capacity : (j + 1) * capacity, :
            ]
        pick = one_hot(table_ref, 0, j, rows, experts * capacity)
        part_ref[j] = mm_tn(pick, line_ref[j])
    sums_ref[...] = jnp.zeros(sums_ref.shape, F32)
    for j in range(parts):
        dy = part_ref[j]
        hat, scale = norm_parts(res_ref[j])
        sums_ref[0:1, :] += jnp.sum(dy * hat, axis=0, keepdims=True)
        sums_ref[1:2, :] += jnp.sum(dy, axis=0, keepdims=True)
        dx = norm_back(hat, scale, gains_ref[2:3, :], dy)
        dx = dx + jnp.where(me_ref[1] == j, cot_ref[...], 0.0)
        dx_ref[j] = dx
        mix_ref[j * rows : (j + 1) * rows, :] = dx.astype(BF)
    group = keep_ref.shape[1]
    for d in range(parts):
        start = pl.multiple_of((me_ref[1] ^ d) * group, group)
        piece = mm_nt(mix_ref[...], proj_ref[pl.ds(start, group), :])
        if d == 0:
            keep_ref[...] = piece
        else:
            send[d - 1][...] = piece.astype(BF)


def combine_out_body(me_ref, table_ref, back_ref, res_ref, own_ref, *refs):
    send, part_ref = refs[:-1], refs[-1]
    experts, slots, width = back_ref.shape
    parts, rows, _ = part_ref.shape
    capacity = slots // parts
    for j in range(parts):
        back = back_ref[:, j * capacity : (j + 1) * capacity, :].reshape(experts * capacity, width)
        gate = gate_hot(table_ref, 2, j, rows, experts * capacity)
        high = gate.astype(BF)
        low = (gate - high.astype(F32)).astype(BF)
        part_ref[j] = mm_tn(high, back) + mm_tn(low, back)
    spread_parts(me_ref[1], part_ref, own_ref, send)
    own_ref[...] += res_ref[...]


def peer_groups(count):
    quarter = count // 4
    half = quarter // 2
    own, near, far, both = [list(range(g * quarter, (g + 1) * quarter)) for g in range(4)]
    return [own, both, far[:half] + near[:half], far[half:] + near[half:]]


def hidden_grad_body(groups, me_ref, g_ref, down_ref, *out_refs):
    rows = g_ref.shape[1]
    for group, out_ref in zip(groups, out_refs):
        for i, d in enumerate(group):
            out_ref[i * rows : (i + 1) * rows, :] = mm(g_ref[me_ref[0] ^ d], down_ref[...])


def expert_body(count, *refs):
    rows_refs = refs[:count]
    gh_ref, up_ref = refs[count : count + 2]
    gr_refs = refs[count + 2 : 2 * count + 2]
    hid_ref, gp_ref, pre_ref = refs[2 * count + 2 :]
    rows = rows_refs[0].shape[0]
    for i in range(count):
        pre_ref[i * rows : (i + 1) * rows, :] = mm(rows_refs[i][...], up_ref[...])
    tile = 32

    def step(j, carry):
        at = pl.ds(pl.multiple_of(j * tile, tile), tile)
        u = pre_ref[at, :]
        sq = u * u
        t = jnp.tanh(C0 * (u + C1 * (sq * u)))
        half = 0.5 * (1.0 + t)
        hid_ref[at, :] = (u * half).astype(BF)
        slope = half + 0.5 * u * (1.0 - t * t) * (C0 * (1.0 + 3.0 * C1 * sq))
        gp_ref[at, :] = (gh_ref[at, :] * slope).astype(BF)
        return carry

    lax.fori_loop(0, count * rows // tile, step, 0)
    for i in range(count):
        gr_refs[i][...] = mm_nt(gp_ref[i * rows : (i + 1) * rows, :], up_ref[...]).astype(BF)


def expert_out_body(groups, me_ref, down_ref, *refs):
    hids, out_ref = refs[:-1], refs[-1]
    rows = out_ref.shape[1]
    for group, hid_ref in zip(groups, hids):
        for i, d in enumerate(group):
            out_ref[me_ref[0] ^ d] = mm_nt(
                hid_ref[i * rows : (i + 1) * rows, :], down_ref[...]
            ).astype(BF)


def grad_up_body(count, *refs):
    lefts, rights, out_ref, temp_ref = refs[: -2 - count], refs[-2 - count : -2], refs[-2], refs[-1]
    rows = lefts[0].shape[0]
    per = len(lefts) // count
    for g in range(count):
        for i in range(per):
            temp_ref[i * rows : (i + 1) * rows, :] = lefts[g * per + i][...]
        piece = mm_tn(temp_ref[...], rights[g][...])
        out_ref[0] = piece if g == 0 else out_ref[0] + piece


def grad_down_body(groups, me_ref, left_ref, *refs):
    rights, out_ref, temp_ref = refs[:-2], refs[-2], refs[-1]
    rows = left_ref.shape[1]
    for g, group in enumerate(groups):
        for i, d in enumerate(group):
            temp_ref[i * rows : (i + 1) * rows, :] = left_ref[me_ref[0] ^ d]
        piece = mm_tn(temp_ref[...], rights[g][...])
        out_ref[0] = piece if g == 0 else out_ref[0] + piece


def local(
    inputs,
    qkv_weight,
    proj_weight,
    first_gain,
    first_shift,
    second_gain,
    second_shift,
    expert_up,
    expert_down,
    gate_logits,
    routes,
    cotangent,
):
    tok, width = inputs.shape
    ns = lax.axis_size("seq")
    nf = lax.axis_size("fsdp")
    group = width // ns
    heads = group // HD
    length = tok * ns
    slots = ns * (4 * tok // nf)
    wrows = qkv_weight.shape[0]
    cols = 3 * group
    hidden = expert_up.shape[2]
    me = jnp.stack([lax.axis_index("fsdp"), lax.axis_index("seq")]).astype(jnp.int32)
    groups = peer_groups(nf)
    per = len(groups[0])
    bf_block = ((tok, width), BF)

    by_group = qkv_weight.reshape(wrows, 3, ns, group).transpose(2, 0, 1, 3).reshape(ns, wrows, cols)
    packed = jnp.concatenate(
        [by_group, jnp.broadcast_to(proj_weight[None], (ns, wrows, width))], axis=2
    )
    gain_row = jnp.concatenate([first_gain, first_shift, second_gain, second_shift])
    gain_row = jnp.pad(gain_row, (0, cols + width - gain_row.shape[0]))
    packed = jnp.concatenate(
        [packed, jnp.broadcast_to(gain_row[None, None, :], (ns, 1, cols + width))], axis=1
    )
    packed = swap(packed, "seq")
    info = jnp.concatenate([routes.astype(F32), gate_logits], axis=1)
    info = jnp.pad(info, ((0, 0), (0, tok - info.shape[1])))
    hat_own, cot_pack = kernel_call(
        prepare_body, [bf_block, ((tok + 2 * INFO, width), BF)], (inputs, cotangent, info)
    )
    cot_pack, packed = lax.optimization_barrier((cot_pack, packed))
    cot_blocks = exchange([cot_pack] * ns, "seq", ns)
    hat_blocks = exchange([hat_own] * ns, "seq", ns)
    first = lax.all_gather(packed[:, :, :cols], "fsdp", axis=0, tiled=True)
    proj_rows, first = lax.optimization_barrier(
        (packed[:, :wrows, cols:].reshape(ns * wrows, width), first)
    )
    qkv_w = first[:, :wrows].reshape(width, cols)
    gains = (
        first[:, wrows, : 4 * wrows]
        .reshape(nf * ns, 4, wrows)
        .transpose(1, 0, 2)
        .reshape(4, width)
        .astype(F32)
    )
    proj_chunks = []
    for piece in exchange([proj_rows] * (nf // 2), "fsdp", nf, stride=2):
        proj_chunks += [piece, lax.ppermute(piece, "fsdp", [(i, i ^ 1) for i in range(nf)])]

    table, stats = kernel_call(
        functools.partial(table_body, nf, slots // ns),
        [((8, length), F32), ((ns, tok, tok), F32)],
        (after(me, qkv_w, gains), *cot_blocks),
        smem=1,
        scratch=[pltpu.VMEM((ns, INFO, tok), F32)],
    )
    (grad_sent,) = kernel_call(
        functools.partial(dispatch_grad_body, ns),
        [((nf, slots, width), BF)],
        (me, table, *cot_blocks),
        smem=1,
        scratch=[pltpu.VMEM((ns, tok, width), BF)],
    )
    grad_in = swap(grad_sent, "fsdp")
    up, down = expert_up[0], expert_down[0]

    hat, attn_in, qkv, heads_s, lse = kernel_call(
        functools.partial(attention_forward_body, heads),
        [
            ((length, width), BF),
            ((length, width), BF),
            ((length, cols), BF),
            ((length, group), BF),
            ((length, 128), F32),
        ],
        (me, gains, qkv_w, *hat_blocks),
        smem=1,
    )
    heads_all = exchange([heads_s] * ns, "seq", ns)
    grad_hidden = kernel_call(
        functools.partial(hidden_grad_body, groups),
        [((per * slots, hidden), F32)] * len(groups),
        (me, grad_in, down),
        smem=1,
    )
    res_all, residual, proj, *sent = kernel_call(
        functools.partial(project_body, ns, nf),
        [((ns, tok, width), F32), ((tok, width), F32), ((width, width), BF)]
        + [((slots, width), BF)] * nf,
        (me, table, hat, stats, inputs, gains, *heads_all, *proj_chunks),
        smem=1,
        scratch=[pltpu.VMEM((length, width), F32), pltpu.VMEM((length, width), BF)],
    )
    rows_in = exchange(sent, "fsdp", nf)
    grad_rows, hid, grad_pre = [None] * nf, [], []
    for g, group_ds in enumerate(groups):
        res = kernel_call(
            functools.partial(expert_body, per),
            [((slots, width), BF)] * per + [((per * slots, hidden), BF)] * 2,
            (*[rows_in[d] for d in group_ds], grad_hidden[g], up),
            scratch=[pltpu.VMEM((per * slots, hidden), F32)],
        )
        for d, piece in zip(group_ds, res):
            grad_rows[d] = piece
        hid.append(res[per])
        grad_pre.append(res[per + 1])
    grad_back = exchange(grad_rows, "fsdp", nf)
    (expert_out,) = kernel_call(
        functools.partial(expert_out_body, groups),
        [((nf, slots, width), BF)],
        (me, down, *hid),
        smem=1,
    )
    temp = [pltpu.VMEM((per * slots, width), BF)]
    (grad_up,) = kernel_call(
        functools.partial(grad_up_body, len(groups)),
        [((1, width, hidden), F32)],
        (*[rows_in[d] for group_ds in groups for d in group_ds], *grad_pre),
        scratch=temp,
    )
    (grad_down,) = kernel_call(
        functools.partial(grad_down_body, groups),
        [((1, width, hidden), F32)],
        (me, grad_in, *hid),
        smem=1,
        scratch=temp,
    )

    image = [pltpu.VMEM((ns, tok, width), F32)]
    share = [((tok, width), F32)] + [bf_block] * (ns - 1)
    grad_res, mix, sums_two, gh_own, *gh_sent = kernel_call(
        functools.partial(combine_grad_body, nf),
        [
            ((ns, tok, width), F32),
            ((length, width), BF),
            ((2, width), F32),
            ((length, group), F32),
        ]
        + [((length, group), BF)] * (ns - 1),
        (me, table, res_all, cotangent, gains, proj, *grad_back),
        smem=1,
        scratch=image + [pltpu.VMEM((ns, nf * slots // ns, width), BF)],
    )
    out_back = swap(after(expert_out, grad_down), "fsdp")
    gh_got = exchange([None] + gh_sent, "seq", ns)[1:]
    grad_qkv, sums_one, grad_own, *grad_share = kernel_call(
        functools.partial(attention_backward_body, heads),
        [((length, cols), BF), ((2, width), F32)] + share,
        (me, gh_own, *gh_got, qkv, lse, qkv_w, hat, stats, gains, grad_res),
        smem=1,
        scratch=image,
    )
    grad_inputs = grad_own
    for piece in exchange([None] + grad_share, "seq", ns)[1:]:
        grad_inputs = grad_inputs + piece.astype(F32)
    wide = ns * wrows
    half = nf // 2

    def over_chips(keep, sent):
        got = lax.ppermute(sent, "fsdp", [(i, i ^ 1) for i in range(nf)])
        both = kernel_call(pair_sum_body, [(keep.shape[1:], BF)] * half, (me, keep, got), smem=1)
        return exchange(both, "fsdp", nf, stride=2)

    keep_p, send_p = kernel_call(
        functools.partial(proj_grad_body, ns),
        [((half, wide, width), F32), ((half, wide, width), BF)],
        (me, mix, *heads_all),
        smem=1,
        scratch=[pltpu.VMEM((width, width), F32), pltpu.VMEM((nf, wide, width), F32)],
    )
    parts_p = over_chips(keep_p, send_p)
    keep_q, send_q = kernel_call(
        weight_grad_body,
        [((half, wide + 8, cols), F32), ((half, wide + 8, cols), BF)],
        (me, attn_in, grad_qkv, sums_one, sums_two),
        smem=1,
        scratch=[pltpu.VMEM((nf, wide, cols), F32), pltpu.VMEM((nf, 8, cols), F32)],
    )
    parts_q = over_chips(keep_q, send_q)
    last = kernel_call(
        functools.partial(last_sum_body, ns, wide, half),
        [((wrows + 8, cols + width), BF)] * ns,
        (me, *parts_q, *parts_p),
        smem=1,
        scratch=[pltpu.VMEM((ns, wrows + 8, cols + width), BF)],
    )
    last = exchange(last, "seq", ns)
    grad_qkv_weight, grad_proj, line = kernel_call(
        functools.partial(last_body, wrows, group),
        [((wrows, 3 * width), F32), ((wrows, width), F32), ((1, 128), F32)],
        (me, *last),
        smem=1,
        scratch=[pltpu.VMEM((ns, wrows + 8, cols + width), BF)],
    )
    tiny = line[0, : 4 * wrows].reshape(4, wrows)
    output, *out_share = kernel_call(
        combine_out_body, share, (me, table, out_back, residual), smem=1, scratch=image
    )
    for piece in exchange([None] + out_share, "seq", ns)[1:]:
        output = output + piece.astype(F32)

    return (
        output,
        grad_inputs,
        grad_qkv_weight,
        grad_proj,
        tiny[0],
        tiny[1],
        tiny[2],
        tiny[3],
        grad_up,
        grad_down,
    )


def solution(mesh):
    both = ("fsdp", "seq")
    rows, line, expert = P(both, None), P(both), P("fsdp", None, "seq")
    in_specs = (rows, rows, rows, line, line, line, line, expert, expert, rows, rows, rows)
    out_specs = (rows, rows, rows, rows, line, line, line, line, expert, expert)
    return jax.shard_map(local, mesh=mesh, in_specs=in_specs, out_specs=out_specs, check_vma=False)
```
